256 devices in a mesh: wide: 32 (over z, y), narrow: 8 (over x, core).
Axes of the slice: x: 4, y: 4, z: 8, core: 2. Of those that a mesh axis runs over, the one named last changes fastest.
Arguments:
- upstream_hot: bfloat16 [524288, 512], P(('wide', 'narrow')), may hold values from -6 to 6
- upstream_warm: bfloat16 [524288, 512], P(('wide', 'narrow')), may hold values from -6 to 6
- upstream_cold: bfloat16 [524288, 512], P(('wide', 'narrow')), may hold values from -6 to 6
- saved_hot: bfloat16 [524288, 512], P(('wide', 'narrow')), may hold values from -6 to 6
- saved_warm: bfloat16 [524288, 128], P(('wide', 'narrow')), may hold values from -6 to 6
- saved_cold: bfloat16 [32, 524288], P(None, ('wide', 'narrow')), may hold values from -6 to 6
- weight_hot: bfloat16 [512, 512], replicated, may hold values from -0.25 to 0.25
- weight_warm: bfloat16 [128, 512], replicated, may hold values from -0.25 to 0.25
- weight_cold: bfloat16 [32, 512], replicated, may hold values from -0.25 to 0.25
- owner_hot: int32 [524288, 1], P(('wide', 'narrow')), may hold values from 0 to 255; in each aligned block of 2048 rows (0 to 2047, 2048 to 4095, ...) at most 16 rows name the same one
- owner_warm: int32 [524288, 1], P(('wide', 'narrow')), may hold values from 0 to 255; in each aligned block of 2048 rows (0 to 2047, 2048 to 4095, ...) at most 16 rows name the same one
- owner_cold: int32 [524288, 1], P(('wide', 'narrow')), may hold values from 0 to 255; in each aligned block of 2048 rows (0 to 2047, 2048 to 4095, ...) at most 16 rows name the same one
- local_hot: int32 [524288], P(('wide', 'narrow')), may hold values from 0 to 511
- local_warm: int32 [524288], P(('wide', 'narrow')), may hold values from 0 to 2047
- local_cold: int32 [524288], P(('wide', 'narrow')), may hold values from 0 to 4095
Outputs:
- table_hot: float32 [131072, 512], P(('wide', 'narrow'))
- table_warm: float32 [524288, 128], P(('wide', 'narrow'))
- table_cold: float32 [32, 1048576], P(None, ('wide', 'narrow'))
- mixing_hot: float32 [512, 512], replicated
- mixing_warm: float32 [128, 512], replicated
- mixing_cold: float32 [32, 512], replicated
The draws below stay inside these ranges and needn't reach their ends.
Inputs may be any that keep to these rules, and one draw needn't show every extreme that they name: `owner_hot`: among the 2048 lookups of the most frequent bucket on one device, at most 16 have the same owner, and that many is reached. `owner_warm`: among the 2048 lookups of the middle bucket on one device, at most 16 have the same owner, and that many is reached. `owner_cold`: among the 2048 lookups of the rarest bucket on one device, at most 16 have the same owner, and that many is reached.
All inputs are finite; a program needn't handle non-finite values.
Results may differ from the reference program's by a relative error of at most 0.0029.
Values may be sent and summed in bfloat16 or wider, within the bound.
A program may use at most 128 MiB of HBM per device.

```python
import math
import jax
import jax.numpy as jnp
import numpy as np

D = 512
W_HOT = 512
W_WARM = 128
W_COLD = 32
LOOK = 2048
ROWS_HOT = 512
ROWS_WARM = 2048
ROWS_COLD = 4096
CAP = 16
LOOKUPS = 524288
N_WIDE = 32
N_NARROW = 8
DEVICES = 256


def set_ends(drawn, rng, least, high):
    place = [jax.random.randint(jax.random.fold_in(rng, axis), (), 0, length) for axis, length in enumerate(drawn.shape)]
    longest = drawn.shape.index(max(drawn.shape))
    neighbour = place[:longest] + [(place[longest] + 1) % drawn.shape[longest]] + place[longest + 1:]
    return drawn.at[tuple(place)].set(least).at[tuple(neighbour)].set(high)


def level_of(key, extent, split, smallest, top_value):
    def one(axis_at, parts):
        draws = jax.random.uniform(jax.random.fold_in(jax.random.fold_in(key, 6), axis_at), (parts,), jnp.float32, smallest / len(split), top_value / len(split))
        return jnp.repeat(jnp.exp(draws), extent[axis_at] // parts).reshape((-1,) + (1,) * (len(extent) - axis_at - 1))

    loudness = one(*split[0])
    for cut in split[1:]:
        loudness = loudness * one(*cut)
    return loudness


def rank_table(count, lean):
    portions = [(1 << 20) // math.isqrt(standing ** lean) + 1 for standing in range(1, count + 1)]
    spread = 1 + sum(portions) // (1 << 30)
    return np.cumsum(np.array([max(1, weight // spread) for weight in portions]))


def skewed_ids(stream_key, dims, amount, skew):
    grid = rank_table(amount, skew)
    ticket = jax.random.randint(jax.random.fold_in(stream_key, 1), dims, 0, int(grid[amount - 1]))
    standing = jnp.searchsorted(jnp.asarray(grid, jnp.int32), ticket, side="right")
    return jax.random.permutation(jax.random.fold_in(stream_key, 2), amount)[standing].astype(jnp.int32)


def deal_out(own_key, own, number, rows, number_of, top, limit, slope):
    ranking = jax.random.permutation(own_key, number_of)
    packed, usual = shares(number_of, rows * top, limit, slope, True), shares(number_of, rows * top, limit, slope, False)
    places = jnp.arange(number_of)

    def named(lengths, offset_by):
        used = int((lengths > 0).sum())
        fixed = max(1, used // 4)
        moved = fixed + (places - fixed + offset_by * (used - fixed)) % max(1, number_of - fixed)
        return jnp.zeros((number_of,), jnp.int32).at[ranking[jnp.where(places < fixed, places, moved)]].set(jnp.asarray(lengths, jnp.int32))

    lengths = jnp.where(number % 4 == 0, named(packed, number // 4), named(usual, number - number // 4 - 1))
    mixed = jax.random.permutation(jax.random.fold_in(own, 3), number_of)
    giver, receiver = mixed[0:number_of // 2 * 2:2], mixed[1:number_of // 2 * 2:2]
    slack = jnp.minimum(lengths[giver] - 1, limit - lengths[receiver]) // 2
    slack = jnp.where((giver == ranking[0]) | (receiver == ranking[0]) | (lengths[receiver] == 0), 0, jnp.maximum(slack, 0))
    moved = jax.random.randint(jax.random.fold_in(own, 4), (number_of // 2,), 0, 1 << 20) % (slack + 1)
    lengths = lengths.at[giver].add(-moved).at[receiver].add(moved)
    items = jnp.searchsorted(jnp.cumsum(lengths), jnp.arange(rows * top), side="right").astype(jnp.int32)
    listing = items.reshape(top, rows).T
    listing = listing[jax.random.permutation(jax.random.fold_in(own, 1), rows)]
    offset_by = jax.random.randint(jax.random.fold_in(own, 2), (rows, 1), 0, top)
    return jnp.take_along_axis(listing, (jnp.arange(top)[None, :] + offset_by) % top, axis=1)


def shares(amount, total, most, lean, full):
    portions = [(1 << 20) // math.isqrt(standing ** lean) + 1 for standing in range(1, amount + 1)]
    largest = most if full else min(most, max(-(-total // amount), total * portions[0] // sum(portions)))
    least = 1 if total - largest >= amount - 1 else 0
    counts, rest = [largest] + [least] * (amount - 1), total - largest - least * (amount - 1)
    while rest > 0:
        free = [i for i in range(1, amount) if counts[i] < largest] or [i for i in range(1, amount) if counts[i] < most]
        whole, budget = sum([portions[i] for i in free]), rest
        for i in free:
            more = min(most - counts[i], max(1, budget * portions[i] // whole), rest)
            counts[i] = counts[i] + more
            rest = rest - more
    return np.array(counts)


def gaussian(key, extent, scale, most, cuts=(), dtype=jnp.bfloat16):
    level = level_of(key, extent, cuts, -0.22, 0.18) if cuts else 1.0
    entries = jax.random.normal(key, extent, jnp.float32) * scale * level
    return jnp.minimum(jnp.maximum(entries, -most), most).astype(dtype)


def setup_inputs(seed: int = 0) -> dict:
    streams_of = jax.random.split(jax.random.key(seed), 16)
    upstream_hot = gaussian(streams_of[0], (LOOKUPS, D), 1.0, 6.0, ((0, 256),))
    upstream_warm = gaussian(streams_of[1], (LOOKUPS, D), 1.0, 6.0, ((0, 256),))
    upstream_cold = gaussian(streams_of[2], (LOOKUPS, D), 1.0, 6.0, ((0, 256),))
    saved_hot = gaussian(streams_of[3], (LOOKUPS, W_HOT), 1.0, 6.0, ((0, 256),))
    saved_warm = gaussian(streams_of[4], (LOOKUPS, W_WARM), 1.0, 6.0, ((0, 256),))
    saved_cold = gaussian(streams_of[5], (W_COLD, LOOKUPS), 1.0, 6.0, ((1, 256),))
    weight_hot = gaussian(streams_of[6], (W_HOT, D), D ** -0.5, 0.25)
    weight_warm = gaussian(streams_of[7], (W_WARM, D), D ** -0.5, 0.25)
    weight_cold = gaussian(streams_of[8], (W_COLD, D), D ** -0.5, 0.25)
    owner_hot_keys = jax.random.split(jax.random.fold_in(streams_of[9], 1), LOOKUPS // LOOK)
    owner_hot_turns = jax.random.permutation(jax.random.fold_in(streams_of[9], 3), LOOKUPS // LOOK)
    owner_hot = jax.vmap(lambda own, number: deal_out(jax.random.fold_in(streams_of[9], 2), own, number, LOOK, DEVICES, 1, CAP, 2))(owner_hot_keys, owner_hot_turns).reshape((LOOKUPS, 1))
    owner_warm_keys = jax.random.split(jax.random.fold_in(streams_of[10], 1), LOOKUPS // LOOK)
    owner_warm_turns = jax.random.permutation(jax.random.fold_in(streams_of[10], 3), LOOKUPS // LOOK)
    owner_warm = jax.vmap(lambda own, number: deal_out(jax.random.fold_in(streams_of[10], 2), own, number, LOOK, DEVICES, 1, CAP, 2))(owner_warm_keys, owner_warm_turns).reshape((LOOKUPS, 1))
    owner_cold_keys = jax.random.split(jax.random.fold_in(streams_of[11], 1), LOOKUPS // LOOK)
    owner_cold_turns = jax.random.permutation(jax.random.fold_in(streams_of[11], 3), LOOKUPS // LOOK)
    owner_cold = jax.vmap(lambda own, number: deal_out(jax.random.fold_in(streams_of[11], 2), own, number, LOOK, DEVICES, 1, CAP, 2))(owner_cold_keys, owner_cold_turns).reshape((LOOKUPS, 1))
    local_hot = set_ends(skewed_ids(streams_of[12], (LOOKUPS,), ROWS_HOT, 2), jax.random.fold_in(streams_of[12], 3), 0, ROWS_HOT - 1).astype(jnp.int32)
    local_warm = set_ends(skewed_ids(streams_of[13], (LOOKUPS,), ROWS_WARM, 2), jax.random.fold_in(streams_of[13], 3), 0, ROWS_WARM - 1).astype(jnp.int32)
    local_cold = set_ends(skewed_ids(streams_of[14], (LOOKUPS,), ROWS_COLD, 2), jax.random.fold_in(streams_of[14], 3), 0, ROWS_COLD - 1).astype(jnp.int32)
    return {"upstream_hot": upstream_hot, "upstream_warm": upstream_warm, "upstream_cold": upstream_cold, "saved_hot": saved_hot, "saved_warm": saved_warm, "saved_cold": saved_cold, "weight_hot": weight_hot, "weight_warm": weight_warm, "weight_cold": weight_cold, "owner_hot": owner_hot, "owner_warm": owner_warm, "owner_cold": owner_cold, "local_hot": local_hot, "local_warm": local_warm, "local_cold": local_cold}


def spread_rows(upstream, weight, owners, local_rows, table_rows):
    terms = jnp.dot(upstream, weight.T, preferred_element_type=jnp.float32).astype(jnp.bfloat16)
    segment = owners[:, 0] * table_rows + local_rows
    return jax.ops.segment_sum(terms.astype(jnp.float32), segment, num_segments=N_WIDE * N_NARROW * table_rows)

def reference(upstream_hot, upstream_warm, upstream_cold, saved_hot, saved_warm, saved_cold, weight_hot, weight_warm, weight_cold, owner_hot, owner_warm, owner_cold, local_hot, local_warm, local_cold):
    table_hot = spread_rows(upstream_hot, weight_hot, owner_hot, local_hot, ROWS_HOT)
    table_warm = spread_rows(upstream_warm, weight_warm, owner_warm, local_warm, ROWS_WARM)
    table_cold = spread_rows(upstream_cold, weight_cold, owner_cold, local_cold, ROWS_COLD).T
    factor = 1.0 / math.sqrt(LOOKUPS)
    mixing_hot = jnp.dot(saved_hot.T, upstream_hot, preferred_element_type=jnp.float32) * factor
    mixing_warm = jnp.dot(saved_warm.T, upstream_warm, preferred_element_type=jnp.float32) * factor
    mixing_cold = jnp.dot(saved_cold, upstream_cold, preferred_element_type=jnp.float32) * factor
    return (table_hot, table_warm, table_cold, mixing_hot, mixing_warm, mixing_cold)
```

```python
import math

import jax
import jax.numpy as jnp
from jax import lax
from jax.experimental import pallas as pl
from jax.experimental.pallas import tpu as pltpu
from jax.sharding import PartitionSpec as P

MESH = pl.DeviceIdType.MESH
BF = jnp.bfloat16
F32 = jnp.float32
I32 = jnp.int32

NZ = 8
NP = 32
CAP = 16
LOOK = 2048
HOT = 2
NT = (((1,), (1,)), ((), ()))
TN = (((0,), (0,)), ((), ()))
PIECE = 192


def dot(a, b, dims=(((1,), (0,)), ((), ()))):
    return lax.dot_general(a, b, dims, preferred_element_type=F32)


def iota(shape, dim):
    return lax.broadcasted_iota(I32, shape, dim)


def one(cond):
    return jnp.where(cond, 1.0, 0.0).astype(BF)


def kernel(
    factor,
    own_h, own_w, own_c, loc_h, loc_w, loc_c,
    a_up_w, a_up_c, a_up_h, a_sv_h, a_sv_w, a_sv_c, a_w_w, a_w_c, a_w_h,
    out_th, out_tw, out_tc, out_mh, out_mw, out_mc,
    up_w, up_c, up_h, sv_h, sv_w, sv_c, w_w, w_c, w_h,
    term_w, term_c, term_h,
    tri, ohk, pick, slots, ls, lr, lz, zl,
    s, r, ohh, ring_l, ring_s, got_l, got_s,
    zw, zc, cs, xw, ohw, lows,
    mp, pair, part, zsum, ypart, ysum, xsum, yall, gall,
    in_sem, lab_send, lab_recv, pl_send, pl_recv, z_send, z_recv,
    rl_send, rs_send, rl_recv, rs_recv, ar_send, ar_recv,
):
    wide, narrow = lax.axis_index("wide"), lax.axis_index("narrow")
    me_z, me_y = lax.div(wide, 4), lax.rem(wide, 4)
    me_x, me_c = lax.div(narrow, 2), lax.rem(narrow, 2)
    me_p = me_y * 8 + narrow
    me_j, me_g = lax.rem(me_p, 4), lax.div(me_p, 4)

    def plane_dev(p):
        return (me_z * 4 + lax.div(p, 8), lax.rem(p, 8))

    def z_dev(z):
        return (z * 4 + me_y, narrow)

    def remote(src, dst, ssem, rsem, dev):
        return pltpu.make_async_remote_copy(
            src_ref=src, dst_ref=dst, send_sem=ssem, recv_sem=rsem, device_id=dev, device_id_type=MESH
        )

    def drain(ref, sem):
        pltpu.make_async_copy(ref, ref, sem).wait()

    loads = []
    for n, (src, dst) in enumerate(
        (
            (a_w_w, w_w), (a_up_w, up_w), (a_w_c, w_c), (a_up_c, up_c), (a_up_h, up_h),
            (a_w_h, w_h), (a_sv_h, sv_h), (a_sv_w, sv_w), (a_sv_c, sv_c),
        )
    ):
        copy = pltpu.make_async_copy(src, dst, in_sem.at[n])
        copy.start()
        loads.append(copy)

    barrier = pltpu.get_barrier_semaphore()

    @pl.loop(1, NP)
    def _(i):
        pl.semaphore_signal(barrier, inc=1, device_id=plane_dev(lax.rem(me_p + i, NP)), device_id_type=MESH)

    @pl.loop(1, NZ)
    def _(i):
        pl.semaphore_signal(barrier, inc=1, device_id=z_dev(lax.rem(me_z + i, NZ)), device_id_type=MESH)

    tri[...] = one(iota((256, 256), 0) < iota((256, 256), 1))

    def keys(b, own_ref, loc_ref):
        run = jnp.zeros((256, 1), F32)
        high = jnp.zeros((256, 128), F32)
        low = jnp.zeros((256, 128), F32)
        for k in range(8):
            cols = slice(k * 256, (k + 1) * 256)
            own = own_ref[:, cols]
            key = (own & 31) * 8 + (own >> 5)
            hit = iota((256, 256), 0) == key
            hit_b = one(hit)
            before = dot(hit_b, tri[...]) + run
            place = jnp.sum(jnp.where(hit, before, 0.0), axis=0, keepdims=True).astype(I32)
            run = run + jnp.sum(jnp.where(hit, 1.0, 0.0), axis=1, keepdims=True)
            slots[b, :, cols] = key * CAP + place
            label = loc_ref[:, cols] + 1
            at = iota((128, 256), 0) == place + me_g * CAP
            high += dot(hit_b, jnp.where(at, (label >> 6).astype(F32), 0.0).astype(BF), NT)
            low += dot(hit_b, jnp.where(at, (label & 63).astype(F32), 0.0).astype(BF), NT)
        ls[b] = (high * 64.0 + low).astype(I32).reshape(NP, NZ, 128)

    keys(0, own_w, loc_w)
    keys(1, own_c, loc_c)
    keys(2, own_h, loc_h)

    def project(up, w, term, mask):
        @pl.loop(0, 8)
        def _(i):
            rows = pl.ds(pl.multiple_of(i * 256, 256), 256)
            t = dot(up[rows, :], w[...], NT)
            if mask:
                t = jnp.where(lax.div(iota((256, 128), 1), 32) == me_j, t, 0.0)
            term[rows, :] = t.astype(BF)

    def pack(b, term, first, chunks):
        @pl.loop(0, NP // 2)
        def _(i):
            q = lax.rem(lax.div(me_p, 2) + i, NP // 2)
            for k in range(8):
                cols = slice(k * 256, (k + 1) * 256)
                pick[:, cols] = one(iota((256, 256), 0) + q * 256 == slots[b, :, cols])
            for n in range(chunks):
                res = dot(pick[...], term[:, n * 128:(n + 1) * 128]) if chunks == 1 else None
                if chunks > 1:
                    if n % 2:
                        continue
                    res = dot(pick[...], term[:, n * 128:(n + 2) * 128])
                    s[first + n + 1, pl.ds(q * 2, 2)] = res[:, 128:].astype(BF).reshape(2, NZ, CAP, 128)
                s[first + n, pl.ds(q * 2, 2)] = res[:, :128].astype(BF).reshape(2, NZ, CAP, 128)

    def send_chunk(k):
        pltpu.make_async_copy(s.at[k, me_p], r.at[k, me_p], pl_recv.at[k]).start()

        @pl.loop(1, NP)
        def _(i):
            p = lax.rem(me_p + i, NP)
            remote(s.at[k, p], r.at[k, me_p], pl_send.at[k], pl_recv.at[k], plane_dev(p)).start()

    loads[0].wait()
    loads[1].wait()
    project(up_w, w_w, term_w, False)
    loads[2].wait()
    loads[3].wait()
    project(up_c, w_c, term_c, True)

    pl.semaphore_wait(barrier, NP - 1 + NZ - 1)
    pltpu.make_async_copy(ls.at[:, me_p], lr.at[:, me_p], lab_recv).start()

    @pl.loop(1, NP)
    def _(i):
        p = lax.rem(me_p + i, NP)
        remote(ls.at[:, p], lr.at[:, me_p], lab_send, lab_recv, plane_dev(p)).start()

    pack(0, term_w, 0, 1)
    send_chunk(0)
    pack(1, term_c, 1, 1)
    send_chunk(1)

    def keep(row, value):
        done = 0
        while done < value.shape[0]:
            block, inside = divmod(row + done, PIECE)
            count = min(PIECE - inside, value.shape[0] - done)
            for lane in range(4):
                mp[block // 2, (block % 2) * 4 + lane, inside:inside + count, :] = value[
                    done:done + count, lane * 128:(lane + 1) * 128
                ]
            done += count

    loads[4].wait()
    loads[6].wait()
    loads[7].wait()
    loads[8].wait()
    for m in range(4):
        keep(m * 128, dot(sv_h[:, m * 128:(m + 1) * 128], up_h[...], TN))
    keep(512, dot(sv_w[...], up_w[...], TN))
    keep(640, dot(sv_c[...], up_c[...]))
    keep(672, jnp.zeros((96, 512), F32))
    other = (wide, me_x * 2 + 1 - me_c)
    remote(mp.at[1 - me_c], pair, ar_send.at[0], ar_recv.at[0], other).start()

    loads[5].wait()
    project(up_h, w_h, term_h, False)
    pack(2, term_h, HOT, 4)
    send_chunk(HOT)
    send_chunk(HOT + 1)

    drain(pair, ar_recv.at[0])
    for q in range(NZ):
        part[q] = mp[me_c, q] + pair[q]
    pltpu.make_async_copy(part.at[me_z], zsum.at[me_z], ar_recv.at[1]).start()

    @pl.loop(1, NZ)
    def _(i):
        z = lax.rem(me_z + i, NZ)
        remote(part.at[z], zsum.at[me_z], ar_send.at[1], ar_recv.at[1], z_dev(z)).start()

    drain(lr, lab_recv)
    for b in range(3):
        for j in range(4):
            row = lr[b, j]
            for g in range(1, 8):
                row = row + lr[b, 4 * g + j]
            for z in range(NZ):
                lz[z, b * 4 + j:b * 4 + j + 1, :] = row[z:z + 1, :]

    @pl.loop(0, NZ)
    def _(t):
        for j in range(4):
            ohh[t, :, j * 128:(j + 1) * 128] = one(iota((512, 128), 0) + 1 == lz[t, 8 + j:9 + j, :])

    drain(r.at[0], pl_recv.at[0])
    pltpu.make_async_copy(r.at[0, :, me_z], zw.at[me_z], z_recv.at[0]).start()
    pltpu.make_async_copy(lz.at[me_z, 0:8], zl.at[me_z], z_recv.at[2]).start()

    @pl.loop(1, NZ)
    def _(i):
        t = lax.rem(me_z + i, NZ)
        remote(r.at[0, :, t], zw.at[me_z], z_send.at[0], z_recv.at[0], z_dev(t)).start()
        remote(lz.at[t, 0:8], zl.at[me_z], z_send.at[2], z_recv.at[2], z_dev(t)).start()

    drain(r.at[1], pl_recv.at[1])

    @pl.loop(0, NZ)
    def _(t):
        for g in range(8):
            total = r[1, 4 * g, t].astype(F32)
            for j in range(1, 4):
                total = total + r[1, 4 * g + j, t].astype(F32)
            cs[t, g] = total.astype(BF)

    pltpu.make_async_copy(cs.at[me_z], zc.at[me_z], z_recv.at[1]).start()

    @pl.loop(1, NZ)
    def _(i):
        t = lax.rem(me_z + i, NZ)
        remote(cs.at[t], zc.at[me_z], z_send.at[1], z_recv.at[1], z_dev(t)).start()

    def mix_y():
        drain(zsum, ar_recv.at[1])
        for y in range(4):
            rows = slice(y * 48, (y + 1) * 48)
            total = zsum[0, rows, :]
            for z in range(1, NZ):
                total = total + zsum[z, rows, :]
            ypart[y] = total
        pltpu.make_async_copy(ypart.at[me_y], ysum.at[me_y], ar_recv.at[2]).start()
        for i in range(1, 4):
            y = lax.rem(me_y + i, 4)
            remote(ypart.at[y], ysum.at[me_y], ar_send.at[2], ar_recv.at[2], (me_z * 4 + y, narrow)).start()

    def mix_x():
        drain(ysum, ar_recv.at[2])
        xsum[4] = ysum[0] + ysum[1] + ysum[2] + ysum[3]
        pltpu.make_async_copy(xsum.at[4], xsum.at[me_x], ar_recv.at[3]).start()
        for i in range(1, 4):
            x = lax.rem(me_x + i, 4)
            remote(xsum.at[4], xsum.at[me_x], ar_send.at[3], ar_recv.at[3], (wide, x * 2 + me_c)).start()

    def mix_y_back():
        drain(xsum.at[0:4], ar_recv.at[3])
        yall[4] = (xsum[0] + xsum[1] + xsum[2] + xsum[3]) * factor
        pltpu.make_async_copy(yall.at[4], yall.at[me_y], ar_recv.at[4]).start()
        for i in range(1, 4):
            y = lax.rem(me_y + i, 4)
            remote(yall.at[4], yall.at[me_y], ar_send.at[4], ar_recv.at[4], (me_z * 4 + y, narrow)).start()

    def mix_z_back():
        drain(yall.at[0:4], ar_recv.at[4])
        pltpu.make_async_copy(yall.at[0:4], gall.at[me_c, me_z], ar_recv.at[5]).start()

        @pl.loop(1, NZ)
        def _(i):
            z = lax.rem(me_z + i, NZ)
            remote(yall.at[0:4], gall.at[me_c, me_z], ar_send.at[5], ar_recv.at[5], z_dev(z)).start()

    def mix_pair_back():
        drain(gall.at[0], ar_recv.at[5])
        remote(gall.at[me_c], gall.at[me_c], ar_send.at[6], ar_recv.at[6], other).start()

    def mix_out():
        drain(gall.at[0], ar_recv.at[6])
        for block in range(4):
            for lane in range(4):
                cols = slice(lane * 128, (lane + 1) * 128)
                for y in range(4):
                    value = gall[block // 2, (block % 2) * 4 + lane, y]
                    row = block * PIECE + y * 48
                    for lo, hi, out in ((0, 512, out_mh), (512, 640, out_mw), (640, 672, out_mc)):
                        begin, end = max(row, lo), min(row + 48, hi)
                        if begin < end:
                            out[begin - lo:end - lo, cols] = value[begin - row:end - row]

    def partial(c, t):
        x = jnp.concatenate([r[HOT + c, 4 * g + j, t] for j in range(4) for g in range(8)], axis=0)
        return dot(ohh[t], x)

    def ring(c, step):
        way = 1 - 2 * lax.rem(me_c + c, 2)
        t = lax.rem(me_z + NZ + way * (4 - step), NZ)
        value = partial(c, t)
        if step:
            drain(got_l.at[c, step - 1], rl_recv.at[c, step - 1])
            value = value + got_l[c, step - 1].astype(F32)
        ring_l[c, step] = value.astype(BF)
        if step:
            t = lax.rem(me_z + NZ - way * (4 - step), NZ)
            value = partial(c, t)
            if step > 1:
                drain(got_s.at[c, step - 2], rs_recv.at[c, step - 2])
                value = value + got_s[c, step - 2].astype(F32)
            ring_s[c, step - 1] = value.astype(BF)
        remote(
            ring_l.at[c, step], got_l.at[c, step], rl_send.at[c, step], rl_recv.at[c, step],
            z_dev(lax.rem(me_z + NZ + way, NZ)),
        ).start()
        if step:
            remote(
                ring_s.at[c, step - 1], got_s.at[c, step - 1], rs_send.at[c, step - 1], rs_recv.at[c, step - 1],
                z_dev(lax.rem(me_z + NZ - way, NZ)),
            ).start()

    def ring_end(c):
        value = partial(c, me_z)
        drain(got_l.at[c, 3], rl_recv.at[c, 3])
        drain(got_s.at[c, 2], rs_recv.at[c, 2])
        out_th[:, c * 128:(c + 1) * 128] = value + got_l[c, 3].astype(F32) + got_s[c, 2].astype(F32)

    def arrive(c):
        drain(r.at[HOT + c], pl_recv.at[HOT + c])

    def warm_table():
        drain(zw, z_recv.at[0])
        drain(zl, z_recv.at[2])

        @pl.loop(0, NZ)
        def _(z):
            for j in range(4):
                rows = pl.ds(pl.multiple_of((z * 4 + j) * 128, 128), 128)
                xw[rows, :] = jnp.concatenate([zw[z, 4 * g + j] for g in range(8)], axis=0)

        @pl.loop(0, 8)
        def _(i):
            for z in range(NZ):
                for j in range(4):
                    k = (z * 4 + j) * 128
                    ohw[:, k:k + 128] = one(iota((256, 128), 0) + (i * 256 + 1) == zl[z, j:j + 1, :])
            out_tw[pl.ds(pl.multiple_of(i * 256, 256), 256), :] = dot(ohw[...], xw[...])

    def cold_table():
        drain(zc, z_recv.at[1])
        turned = []
        for j in range(4):
            choose = one(iota((32, 128), 1) == iota((32, 128), 0) + 32 * j)
            turned.append(dot(choose, zc[...].reshape(1024, 128), NT))
            for z in range(NZ):
                k = j * 1024 + z * 128
                lows[:, k:k + 128] = one(iota((128, 128), 0) == ((zl[z, 4 + j:5 + j, :] - 1) & 127))
        for h in range(4):
            for j in range(4):
                for z in range(NZ):
                    k = j * 1024 + z * 128
                    high = (zl[z, 4 + j:5 + j, :] - 1) >> 7
                    for i in range(8):
                        ohw[i * 32:(i + 1) * 32, k:k + 128] = jnp.where(
                            high == h * 8 + i, turned[j][:, z * 128:(z + 1) * 128], 0.0
                        ).astype(BF)
            res = dot(ohw[...], lows[...], NT)
            for i in range(8):
                out_tc[:, (h * 8 + i) * 128:(h * 8 + i + 1) * 128] = res[i * 32:(i + 1) * 32, :]

    arrive(0)
    send_chunk(HOT + 2)
    ring(0, 0)
    mix_y()
    ring(0, 1)
    ring(0, 2)
    mix_x()
    arrive(1)
    send_chunk(HOT + 3)
    ring(1, 0)
    ring(0, 3)
    mix_y_back()
    ring(1, 1)
    ring_end(0)
    ring(1, 2)
    warm_table()
    arrive(2)
    ring(2, 0)
    ring(1, 3)
    mix_z_back()
    ring(2, 1)
    ring_end(1)
    ring(2, 2)
    cold_table()
    arrive(3)
    ring(3, 0)
    ring(2, 3)
    mix_pair_back()
    ring(3, 1)
    ring_end(2)
    ring(3, 2)
    mix_out()
    ring(3, 3)

    for k in range(6):
        drain(r.at[k, 0:NP - 1], pl_send.at[k])
    drain(lr.at[:, 0:NP - 1], lab_send)
    drain(zw.at[0:NZ - 1], z_send.at[0])
    drain(zc.at[0:NZ - 1], z_send.at[1])
    drain(zl.at[0:NZ - 1], z_send.at[2])
    drain(pair, ar_send.at[0])
    drain(zsum.at[0:NZ - 1], ar_send.at[1])
    drain(ysum.at[0:3], ar_send.at[2])
    drain(xsum.at[0:3], ar_send.at[3])
    drain(yall.at[0:3], ar_send.at[4])
    drain(gall.at[0, 0:NZ - 1], ar_send.at[5])
    drain(gall.at[0], ar_send.at[6])
    for c in range(4):
        for step in range(4):
            drain(got_l.at[c, step], rl_send.at[c, step])
        for step in range(3):
            drain(got_s.at[c, step], rs_send.at[c, step])
    ring_end(3)


def per_device(
    upstream_hot, upstream_warm, upstream_cold, saved_hot, saved_warm, saved_cold,
    weight_hot, weight_warm, weight_cold, owner_hot, owner_warm, owner_cold,
    local_hot, local_warm, local_cold,
):
    devices = lax.axis_size("wide") * lax.axis_size("narrow")
    factor = 1.0 / math.sqrt(LOOK * devices)
    rows = [a.reshape(1, LOOK) for a in (owner_hot, owner_warm, owner_cold, local_hot, local_warm, local_cold)]
    anywhere = pl.BlockSpec(memory_space=pl.ANY)
    near = pl.BlockSpec(memory_space=pltpu.VMEM)
    dma = pltpu.SemaphoreType.DMA
    v = pltpu.VMEM

    def body(*refs):
        kernel(factor, *refs)

    return pl.pallas_call(
        body,
        out_shape=(
            jax.ShapeDtypeStruct((512, 512), F32),
            jax.ShapeDtypeStruct((2048, 128), F32),
            jax.ShapeDtypeStruct((32, 4096), F32),
            jax.ShapeDtypeStruct((512, 512), F32),
            jax.ShapeDtypeStruct((128, 512), F32),
            jax.ShapeDtypeStruct((32, 512), F32),
        ),
        in_specs=[near] * 6 + [anywhere] * 9,
        out_specs=(near,) * 6,
        scratch_shapes=[
            v((2048, 512), BF), v((2048, 512), BF), v((2048, 512), BF),
            v((2048, 512), BF), v((2048, 128), BF), v((32, 2048), BF),
            v((128, 512), BF), v((128, 512), BF), v((512, 512), BF),
            v((2048, 128), BF), v((2048, 128), BF), v((2048, 512), BF),
            v((256, 256), BF), v((8, 128), BF), v((256, 2048), BF), v((3, 1, 2048), I32),
            v((3, NP, NZ, 128), I32), v((3, NP, NZ, 128), I32), v((NZ, 16, 128), I32), v((NZ, 8, 128), I32),
            v((6, NP, NZ, CAP, 128), BF), v((6, NP, NZ, CAP, 128), BF), v((NZ, 512, 512), BF),
            v((4, 4, 512, 128), BF), v((4, 3, 512, 128), BF), v((4, 4, 512, 128), BF), v((4, 3, 512, 128), BF),
            v((NZ, NP, CAP, 128), BF), v((NZ, 8, CAP, 128), BF), v((NZ, 8, CAP, 128), BF),
            v((4096, 128), BF), v((256, 4096), BF), v((128, 4096), BF),
            v((2, NZ, PIECE, 128), F32), v((NZ, PIECE, 128), F32), v((NZ, PIECE, 128), F32), v((NZ, PIECE, 128), F32),
            v((4, 48, 128), F32), v((4, 48, 128), F32), v((5, 48, 128), F32), v((5, 48, 128), F32),
            v((2, NZ, 4, 48, 128), F32),
            dma((9,)), dma(()), dma(()), dma((6,)), dma((6,)), dma((3,)), dma((3,)),
            dma((4, 4)), dma((4, 3)), dma((4, 4)), dma((4, 3)), dma((7,)), dma((7,)),
        ],
        compiler_params=pltpu.CompilerParams(
            collective_id=0, has_side_effects=True, vmem_limit_bytes=67_000_000
        ),
    )(
        *rows,
        upstream_warm, upstream_cold, upstream_hot, saved_hot, saved_warm, saved_cold,
        weight_warm, jnp.tile(weight_cold, (4, 1)), weight_hot,
    )


def solution(mesh):
    both = ("wide", "narrow")
    placed = (
        P(both, None), P(both, None), P(both, None), P(both, None), P(both, None), P(None, both),
        P(), P(), P(),
        P(both, None), P(both, None), P(both, None), P(both), P(both), P(both),
    )
    return jax.shard_map(
        per_device,
        mesh=mesh,
        in_specs=placed,
        out_specs=(P(both, None), P(both, None), P(None, both), P(), P(), P()),
        check_vma=False,
    )
```

```python
import math

import jax
import jax.numpy as jnp
from jax import lax
from jax.experimental import pallas as pl
from jax.experimental.pallas import tpu as pltpu
from jax.sharding import PartitionSpec as P

MESH = pl.DeviceIdType.MESH
BF = jnp.bfloat16
F32 = jnp.float32
I32 = jnp.int32

NZ = 8
NP = 32
CAP = 16
LOOK = 2048
HOT = 1
COLD = 5
NT = (((1,), (1,)), ((), ()))
TN = (((0,), (0,)), ((), ()))
PIECE = 384


def dot(a, b, dims=(((1,), (0,)), ((), ()))):
    return lax.dot_general(a, b, dims, preferred_element_type=F32)


def iota(shape, dim):
    return lax.broadcasted_iota(I32, shape, dim)


def one(cond):
    return jnp.where(cond, 1.0, 0.0).astype(BF)


def kernel(
    factor,
    own_h, own_w, own_c, loc_h, loc_w, loc_c,
    a_up_w, a_up_c, a_up_h, a_sv_h, a_sv_w, a_sv_c, a_w_w, a_w_c, a_w_h,
    hbm_th, hbm_tw, hbm_tc, hbm_mh, hbm_mw, hbm_mc,
    out_th, out_tw, out_tc, out_mh, out_mw, out_mc,
    up_w, up_c, up_h, sv_h, sv_w, sv_c, w_w, w_c, w_h,
    term_w, term_c, term_h,
    tri, pick, slots, ls, lr, lz, zl,
    s, r, s_c, r_c, ohh, ring_l, ring_s, got_l, got_s,
    zw, zc, cs, xw, ohw, lows,
    mp, pair, part, bsum, bpart, ssum, spart, zsum, total, sall, gall,
    in_sem, out_sem, lab_send, lab_recv, pl_send, pl_recv, z_send, z_recv,
    rl_send, rs_send, rl_recv, rs_recv, ar_send, ar_recv,
):
    wide, narrow = lax.axis_index("wide"), lax.axis_index("narrow")
    me_z, me_y = lax.div(wide, 4), lax.rem(wide, 4)
    me_x, me_c = lax.div(narrow, 2), lax.rem(narrow, 2)
    me_p = me_y * 8 + narrow
    other = (wide, me_x * 2 + 1 - me_c)

    def plane_dev(p):
        return (me_z * 4 + lax.div(p, 8), lax.rem(p, 8))

    def z_dev(z):
        return (z * 4 + me_y, narrow)

    def chip(i):
        x, y = me_x + lax.rem(i, 4), me_y + i + lax.div(i, 4)
        return lax.rem(y, 4) * 4 + lax.rem(x, 4)

    def to_peers(send):
        send(me_p + 1 - 2 * me_c)

        @pl.loop(1, NP // 2)
        def _(i):
            send(chip(i) * 2)
            send(chip(i) * 2 + 1)

    def remote(src, dst, ssem, rsem, dev):
        return pltpu.make_async_remote_copy(
            src_ref=src, dst_ref=dst, send_sem=ssem, recv_sem=rsem, device_id=dev, device_id_type=MESH
        )

    def drain(ref, sem):
        pltpu.make_async_copy(ref, ref, sem).wait()

    loads = {}
    for n, (name, src, dst) in enumerate(
        (
            ("w_w", a_w_w, w_w), ("up_w", a_up_w, up_w), ("up_h", a_up_h, up_h), ("sv_h", a_sv_h, sv_h),
            ("sv_w", a_sv_w, sv_w), ("up_c", a_up_c, up_c), ("sv_c", a_sv_c, sv_c), ("w_h", a_w_h, w_h),
            ("w_c", a_w_c, w_c),
        )
    ):
        loads[name] = pltpu.make_async_copy(src, dst, in_sem.at[n])
        loads[name].start()

    barrier = pltpu.get_barrier_semaphore()

    @pl.loop(1, NP)
    def _(i):
        pl.semaphore_signal(barrier, inc=1, device_id=plane_dev(lax.rem(me_p + i, NP)), device_id_type=MESH)

    @pl.loop(1, NZ)
    def _(i):
        pl.semaphore_signal(barrier, inc=1, device_id=z_dev(lax.rem(me_z + i, NZ)), device_id_type=MESH)

    def exact(values):
        return values.astype(F32).astype(BF)

    def match(row, rows=256):
        return jnp.where(exact(iota((rows, row.shape[1]), 0)) == row, jnp.ones((), BF), jnp.zeros((), BF))

    def near(row, base):
        return exact(jnp.clip(row - base, -1, 256))

    def keys(b, own_ref, loc_ref):
        own, label = own_ref[...], loc_ref[...] + 1
        key = exact((own & 31) * 8 + (own >> 5))
        if b < 2:
            base = ((own & 31) * 8 + (own >> 5)) * CAP
        else:
            base = (own & 31) * 128 + (((own >> 5) + me_p) & 7) * CAP
        high, low = exact(label >> 6), exact(label & 63)
        lane = exact(iota((128, 256), 0) & 15)
        none = jnp.zeros((), BF)
        run = jnp.zeros((256, 128), F32)
        both = jnp.zeros((256, 256), F32)
        for k in range(8):
            cols = slice(k * 256, (k + 1) * 256)
            hit = match(key[:, cols])
            count = dot(hit, tri[...])
            before = count[:, 0:256] + jnp.concatenate([run, run], axis=1)
            run = run + count[:, 256:384]
            place = jnp.sum(before * hit.astype(F32), axis=0, keepdims=True)
            slots[b, :, cols] = base[:, cols] + place.astype(I32)
            at = lane == place.astype(BF)
            parts = [jnp.where(at, high[:, cols], none), jnp.where(at, low[:, cols], none)]
            both += dot(hit, jnp.concatenate(parts, axis=0), NT)
        found = both[:, 0:128] * 64.0 + both[:, 128:]
        block = ((iota((256, 128), 0) & 7) + me_p) & 7
        found = jnp.where((iota((256, 128), 1) >> 4) == block, found, 0.0)
        ls[b] = jnp.sum(found.reshape(NP, NZ, 128), axis=1, keepdims=True).astype(I32)

    def project(up, w, term):
        @pl.loop(0, 2)
        def _(i):
            rows = pl.ds(pl.multiple_of(i * 1024, 1024), 1024)
            term[rows, :] = dot(up[rows, :], w[...], NT).astype(BF)

    def send_one(k, p):
        remote(s.at[k, p], r.at[k, me_p], pl_send.at[k], pl_recv.at[k], plane_dev(p)).start()

    def picks(b, q):
        for k in range(8):
            cols = slice(k * 256, (k + 1) * 256)
            pick[:, cols] = match(near(slots[b, :, cols], q * 256))

    def pack(b, term, first, chunks, extra=None):
        @pl.loop(0, NP // 2)
        def _(i):
            q = chip(i)
            picks(b, q)
            for n in range(0, chunks, 2):
                width = min(2, chunks - n)
                if width == 1:
                    res = dot(pick[:, :1024], term[:1024]) + dot(pick[:, 1024:], term[1024:])
                else:
                    res = dot(pick[...], term[:, n * 128:(n + width) * 128])
                res = res.astype(BF)
                for m in range(width):
                    s[first + n + m, pl.ds(q * 2, 2)] = res[:, m * 128:(m + 1) * 128].reshape(2, NZ, CAP, 128)

            @pl.when(i > 1)
            def _():
                last = chip(i - 1)
                send_one(first, last * 2)
                send_one(first, last * 2 + 1)

            if extra is not None:
                pl.when(i == 5)(extra)

        final = chip(NP // 2 - 1)
        pltpu.make_async_copy(s.at[first, me_p], r.at[first, me_p], pl_recv.at[first]).start()
        send_one(first, me_p + 1 - 2 * me_c)
        send_one(first, final * 2)
        send_one(first, final * 2 + 1)

    def pack_cold(part):
        if part == 0:
            loads["w_c"].wait()
            term_c[...] = dot(w_c[...], up_c[...], NT).astype(BF)

        @pl.loop(part * 4, part * 4 + 4)
        def _(i):
            q = chip(i)
            picks(2, q)
            res = dot(term_c[...], pick[...], NT).astype(BF)
            s_c[q * 2] = res[:, :128]
            s_c[q * 2 + 1] = res[:, 128:]

    def send_cold():
        pltpu.make_async_copy(s_c.at[me_p], r_c.at[me_p], pl_recv.at[COLD]).start()

        to_peers(
            lambda p: remote(
                s_c.at[p], r_c.at[me_p], pl_send.at[COLD], pl_recv.at[COLD], plane_dev(p)
            ).start()
        )

    def send_chunk(k):
        pltpu.make_async_copy(s.at[k, me_p], r.at[k, me_p], pl_recv.at[k]).start()

        to_peers(lambda p: send_one(k, p))

    def send_labels(n, lo, hi):
        pltpu.make_async_copy(ls.at[lo:hi, me_p], lr.at[lo:hi, me_p], lab_recv.at[n]).start()

        to_peers(
            lambda p: remote(
                ls.at[lo:hi, p], lr.at[lo:hi, me_p], lab_send.at[n], lab_recv.at[n], plane_dev(p)
            ).start()
        )

    def keep(row, value):
        done = 0
        while done < value.shape[0]:
            half, inside = divmod(row + done, PIECE)
            count = min(PIECE - inside, value.shape[0] - done)
            for lane in range(4):
                mp[half, lane, inside:inside + count, :] = value[done:done + count, lane * 128:(lane + 1) * 128]
            done += count

    def mix_terms():
        for name in ("up_h", "sv_h", "sv_w", "up_c", "sv_c"):
            loads[name].wait()
        for m in range(4):
            keep(m * 128, dot(sv_h[:, m * 128:(m + 1) * 128], up_h[...], TN))
        keep(512, dot(sv_w[...], up_w[...], TN))
        keep(640, dot(sv_c[...], up_c[...]))
        keep(672, jnp.zeros((96, 512), F32))

    def mix_pair():
        remote(mp.at[1 - me_c], pair, ar_send.at[0], ar_recv.at[0], other).start()

    me_a = me_x + me_c * (me_y - me_x)
    me_b = me_y + me_c * (me_x - me_y)

    def a_dev(k):
        return (me_z * 4 + me_y + me_c * (k - me_y), (k + me_c * (me_x - k)) * 2 + me_c)

    def b_dev(k):
        return (me_z * 4 + k + me_c * (me_y - k), (me_x + me_c * (k - me_x)) * 2 + me_c)

    def spread(n, src_of, dst, dev, me, count):
        pltpu.make_async_copy(src_of(me), dst, ar_recv.at[n]).start()

        @pl.loop(1, count)
        def _(i):
            k = lax.rem(me + i, count)
            remote(src_of(k), dst, ar_send.at[n], ar_recv.at[n], dev(k)).start()

    def mix_big():
        drain(pair, ar_recv.at[0])
        for k in range(4):
            part[k] = mp[me_c, k] + pair[k]
        spread(1, lambda k: part.at[k], bsum.at[me_a], a_dev, me_a, 4)

    def mix_small():
        drain(bsum, ar_recv.at[1])
        for k in range(4):
            rows = slice(k * 96, (k + 1) * 96)
            bpart[k] = bsum[0, rows] + bsum[1, rows] + bsum[2, rows] + bsum[3, rows]
        spread(2, lambda k: bpart.at[k], ssum.at[me_b], b_dev, me_b, 4)

    def mix_z():
        drain(ssum, ar_recv.at[2])
        spart[...] = (ssum[0] + ssum[1] + ssum[2] + ssum[3]).astype(BF)
        spread(3, lambda k: spart, zsum.at[me_z], z_dev, me_z, NZ)

    def mix_small_back():
        drain(zsum, ar_recv.at[3])
        added = zsum[0].astype(F32)
        for z in range(1, NZ):
            added = added + zsum[z].astype(F32)
        total[...] = added * factor
        spread(4, lambda k: total, sall.at[me_b], b_dev, me_b, 4)

    def mix_big_back():
        drain(sall, ar_recv.at[4])
        spread(5, lambda k: sall, gall.at[me_c, me_a], a_dev, me_a, 4)

    def mix_pair_back():
        drain(gall.at[0], ar_recv.at[5])
        remote(gall.at[me_c], gall.at[me_c], ar_send.at[6], ar_recv.at[6], other).start()

    def mix_out():
        drain(gall.at[0], ar_recv.at[6])
        for half in range(2):
            for lane in range(4):
                cols = slice(lane * 128, (lane + 1) * 128)
                for b in range(4):
                    value = gall[half, lane, b]
                    row = half * PIECE + b * 96
                    for lo, hi, out in ((0, 512, out_mh), (512, 640, out_mw), (640, 672, out_mc)):
                        begin, end = max(row, lo), min(row + 96, hi)
                        if begin < end:
                            out[begin - lo:end - lo, cols] = value[begin - row:end - row]

    def sort_labels(b):
        lz[b] = jnp.zeros((NZ, 8, 128), I32)
        block, z_at = iota((NZ, 128), 1) >> 4, iota((NZ, 128), 0)
        for j in range(4):
            row = jnp.zeros((NZ, 128), I32)
            for p in range(8):
                row = row + jnp.where(block == ((z_at + p) & 7), lr[b, 8 * j + p], 0)
            for z in range(NZ):
                lz[b, z, j:j + 1, :] = row[z:z + 1, :]

    def hot_rows():
        @pl.loop(0, NZ)
        def _(t):
            for j in range(4):
                row = lz[1, t, j:j + 1, :] - 1
                for half in range(2):
                    ohh[t, half * 256:(half + 1) * 256, j * 128:(j + 1) * 128] = match(near(row, half * 256))

    def labels_on(b, n):
        spread_z(lambda t: lz.at[b, t], zl.at[n, me_z], z_send.at[2 + n], z_recv.at[2 + n])

    def spread_z(src_of, dst, ssem, rsem):
        pltpu.make_async_copy(src_of(me_z), dst, rsem).start()

        @pl.loop(1, NZ)
        def _(i):
            t = lax.rem(me_z + i, NZ)
            remote(src_of(t), dst, ssem, rsem, z_dev(t)).start()

    def warm_on():
        drain(r.at[0], pl_recv.at[0])
        spread_z(lambda t: r.at[0, :, t], zw.at[me_z], z_send.at[0], z_recv.at[0])

    def cold_on():
        drain(r_c, pl_recv.at[COLD])

        @pl.loop(0, NZ)
        def _(t):
            for j in range(4):
                parts = [
                    jnp.where((iota((32, 128), 1) >> 4) == ((t + p) & 7), r_c[8 * j + p].astype(F32), 0.0)
                    for p in range(8)
                ]
                cs[t, :, j * 128:(j + 1) * 128] = sum(parts).astype(BF)

        spread_z(lambda t: cs.at[t], zc.at[me_z], z_send.at[1], z_recv.at[1])

    def leave(n, src, dst):
        copy = pltpu.make_async_copy(src, dst, out_sem.at[n])
        copy.start()
        leaving.append(copy)

    leaving = []

    def partial(c, t):
        x = jnp.concatenate(
            [r[HOT + c, 8 * j + lax.rem(i + NZ - t, NZ), t] for j in range(4) for i in range(8)], axis=0
        )
        return dot(ohh[t], x)

    def ring(c, step):
        way = 1 - 2 * lax.rem(me_c + c, 2)
        value = partial(c, lax.rem(me_z + NZ + way * (4 - step), NZ))
        if step:
            drain(got_l.at[c, step - 1], rl_recv.at[c, step - 1])
            value = value + got_l[c, step - 1].astype(F32)
        ring_l[c, step] = value.astype(BF)
        if step:
            value = partial(c, lax.rem(me_z + NZ - way * (4 - step), NZ))
            if step > 1:
                drain(got_s.at[c, step - 2], rs_recv.at[c, step - 2])
                value = value + got_s[c, step - 2].astype(F32)
            ring_s[c, step - 1] = value.astype(BF)
        remote(
            ring_l.at[c, step], got_l.at[c, step], rl_send.at[c, step], rl_recv.at[c, step],
            z_dev(lax.rem(me_z + NZ + way, NZ)),
        ).start()
        if step:
            remote(
                ring_s.at[c, step - 1], got_s.at[c, step - 1], rs_send.at[c, step - 1], rs_recv.at[c, step - 1],
                z_dev(lax.rem(me_z + NZ - way, NZ)),
            ).start()

    def ring_end(c):
        value = partial(c, me_z)
        drain(got_l.at[c, 3], rl_recv.at[c, 3])
        drain(got_s.at[c, 2], rs_recv.at[c, 2])
        cols = slice(c * 128, (c + 1) * 128)
        out_th[:, cols] = value + got_l[c, 3].astype(F32) + got_s[c, 2].astype(F32)
        leave(c, out_th.at[:, cols], hbm_th.at[:, cols])

    def arrive(c):
        drain(r.at[HOT + c], pl_recv.at[HOT + c])

    def warm_table(half):
        if half == 0:
            drain(zw, z_recv.at[0])
            drain(zl.at[0], z_recv.at[2])

            @pl.loop(0, NZ)
            def _(z):
                for j in range(4):
                    rows = pl.ds(pl.multiple_of((z * 4 + j) * 128, 128), 128)
                    xw[rows, :] = jnp.concatenate(
                        [zw[z, 8 * j + lax.rem(i + NZ - me_z, NZ)] for i in range(8)], axis=0
                    )

        @pl.loop(half * 4, half * 4 + 4)
        def _(i):
            for z in range(NZ):
                for j in range(4):
                    k = (z * 4 + j) * 128
                    ohw[:, k:k + 128] = match(near(zl[0, z, j:j + 1, :] - 1, i * 256))
            res = dot(ohw[:, :2048], xw[:2048]) + dot(ohw[:, 2048:], xw[2048:])
            out_tw[pl.ds(pl.multiple_of(i * 256, 256), 256), :] = res

        if half:
            leave(4, out_tw, hbm_tw)

    def cold_table():
        drain(zc, z_recv.at[1])
        drain(zl.at[1], z_recv.at[3])
        for z in range(NZ):
            for j in range(4):
                k = (z * 4 + j) * 128
                lows[:, k:k + 128] = match(exact((zl[1, z, j:j + 1, :] - 1) & 127), 128)

        @pl.loop(0, 4)
        def _(h):
            for z in range(NZ):
                for j in range(4):
                    k = (z * 4 + j) * 128
                    high = near((zl[1, z, j:j + 1, :] - 1) >> 7, h * 8)
                    for i in range(8):
                        here = jnp.broadcast_to(high, (32, 128)) == jnp.full((), i, BF)
                        ohw[i * 32:(i + 1) * 32, k:k + 128] = jnp.where(
                            here, zc[z, :, j * 128:(j + 1) * 128], jnp.zeros((), BF)
                        )
            res = dot(ohw[:, :2048], lows[:, :2048], NT) + dot(ohw[:, 2048:], lows[:, 2048:], NT)
            for i in range(8):
                out_tc[:, pl.ds(pl.multiple_of(h * 1024 + i * 128, 128), 128)] = res[i * 32:(i + 1) * 32, :]

        leave(5, out_tc, hbm_tc)

    tri[:, 0:256] = one(iota((256, 256), 0) < iota((256, 256), 1))
    tri[:, 256:384] = jnp.ones((256, 128), BF)
    keys(0, own_w, loc_w)
    loads["w_w"].wait()
    loads["up_w"].wait()
    project(up_w, w_w, term_w)
    mix_terms()
    pl.semaphore_wait(barrier, NP - 1 + NZ - 1)
    mix_pair()
    pack(0, term_w, 0, 1)
    keys(1, own_h, loc_h)
    send_labels(0, 0, 2)
    loads["w_h"].wait()
    project(up_h, w_h, term_h)
    mix_big()
    pack(1, term_h, HOT, 4, warm_on)
    mix_small()
    send_chunk(HOT + 1)
    drain(lr.at[0:2], lab_recv.at[0])
    sort_labels(0)
    labels_on(0, 0)
    sort_labels(1)
    hot_rows()
    keys(2, own_c, loc_c)
    pack_cold(0)
    arrive(0)
    ring(0, 0)
    send_chunk(HOT + 2)
    send_labels(1, 2, 3)
    pack_cold(1)
    ring(0, 1)
    pack_cold(2)
    pack_cold(3)
    ring(0, 2)
    mix_z()
    arrive(1)
    ring(1, 0)
    send_chunk(HOT + 3)
    ring(0, 3)
    ring(1, 1)
    ring(1, 2)
    mix_small_back()
    arrive(2)
    ring(2, 0)
    send_cold()
    ring(1, 3)
    ring(2, 1)
    warm_table(0)
    ring(2, 2)
    mix_big_back()
    ring_end(0)
    arrive(3)
    ring(3, 0)
    ring(2, 3)
    drain(lr.at[2], lab_recv.at[1])
    sort_labels(2)
    labels_on(2, 1)
    ring(3, 1)
    warm_table(1)
    ring(3, 2)
    mix_pair_back()
    cold_on()
    ring(3, 3)
    ring_end(1)
    ring_end(2)
    mix_out()
    leave(6, out_mh, hbm_mh)
    leave(7, out_mw, hbm_mw)
    leave(8, out_mc, hbm_mc)
    cold_table()

    for k in range(5):
        drain(r.at[k, 0:NP - 1], pl_send.at[k])
    drain(r_c.at[0:NP - 1], pl_send.at[COLD])
    drain(lr.at[0:2, 0:NP - 1], lab_send.at[0])
    drain(lr.at[2, 0:NP - 1], lab_send.at[1])
    drain(zw.at[0:NZ - 1], z_send.at[0])
    drain(zc.at[0:NZ - 1], z_send.at[1])
    drain(zl.at[0, 0:NZ - 1], z_send.at[2])
    drain(zl.at[1, 0:NZ - 1], z_send.at[3])
    drain(pair, ar_send.at[0])
    drain(bsum.at[0:3], ar_send.at[1])
    drain(ssum.at[0:3], ar_send.at[2])
    drain(zsum.at[0:NZ - 1], ar_send.at[3])
    drain(sall.at[0:3], ar_send.at[4])
    drain(gall.at[0, 0:3], ar_send.at[5])
    drain(gall.at[0], ar_send.at[6])
    for c in range(4):
        for step in range(4):
            drain(got_l.at[c, step], rl_send.at[c, step])
        for step in range(3):
            drain(got_s.at[c, step], rs_send.at[c, step])
    ring_end(3)
    for copy in leaving:
        copy.wait()


def write_out(*refs):
    ins, outs, rooms, (sem,) = refs[:6], refs[6:12], refs[12:18], refs[18:]
    copies = []
    n = 0
    for src, room, dst in zip(ins, rooms, outs):
        cuts = 4 if src.shape[0] >= 256 else 1
        rows = src.shape[0] // cuts
        for k in range(cuts):
            here = pl.ds(k * rows, rows)
            first = pltpu.make_async_copy(src.at[here], room.at[here], sem.at[n])
            second = pltpu.make_async_copy(room.at[here], dst.at[here], sem.at[n + 1])
            first.start()
            copies.append((first, second))
            n += 2
    for first, second in copies:
        first.wait()
        second.start()
    for _, second in copies:
        second.wait()


def per_device(
    upstream_hot, upstream_warm, upstream_cold, saved_hot, saved_warm, saved_cold,
    weight_hot, weight_warm, weight_cold, owner_hot, owner_warm, owner_cold,
    local_hot, local_warm, local_cold,
):
    devices = lax.axis_size("wide") * lax.axis_size("narrow")
    factor = 1.0 / math.sqrt(LOOK * devices)
    rows = [a.reshape(1, LOOK) for a in (owner_hot, owner_warm, owner_cold, local_hot, local_warm, local_cold)]
    anywhere = pl.BlockSpec(memory_space=pl.ANY)
    near = pl.BlockSpec(memory_space=pltpu.VMEM)
    dma = pltpu.SemaphoreType.DMA
    v = pltpu.VMEM
    results = tuple(
        jax.ShapeDtypeStruct(shape, F32)
        for shape in ((512, 512), (2048, 128), (32, 4096), (512, 512), (128, 512), (32, 512))
    )

    def body(*refs):
        kernel(factor, *refs)

    found = pl.pallas_call(
        body,
        out_shape=results,
        in_specs=[near] * 6 + [anywhere] * 9,
        out_specs=(anywhere,) * 6,
        scratch_shapes=[
            *(v(a.shape, F32) for a in results),
            v((2048, 512), BF), v((2048, 512), BF), v((2048, 512), BF),
            v((2048, 512), BF), v((2048, 128), BF), v((32, 2048), BF),
            v((128, 512), BF), v((32, 512), BF), v((512, 512), BF),
            v((2048, 128), BF), v((32, 2048), BF), v((2048, 512), BF),
            v((256, 384), BF), v((256, 2048), BF), v((3, 1, 2048), I32),
            v((3, NP, 1, 128), I32), v((3, NP, 1, 128), I32), v((3, NZ, 8, 128), I32), v((2, NZ, 8, 128), I32),
            v((5, NP, NZ, CAP, 128), BF), v((5, NP, NZ, CAP, 128), BF), v((NP, 32, 128), BF), v((NP, 32, 128), BF),
            v((NZ, 512, 512), BF),
            v((4, 4, 512, 128), BF), v((4, 3, 512, 128), BF), v((4, 4, 512, 128), BF), v((4, 3, 512, 128), BF),
            v((NZ, NP, CAP, 128), BF), v((NZ, 32, 512), BF), v((NZ, 32, 512), BF),
            v((4096, 128), BF), v((256, 4096), BF), v((128, 4096), BF),
            v((2, 4, PIECE, 128), F32), v((4, PIECE, 128), F32), v((4, PIECE, 128), F32), v((4, PIECE, 128), F32),
            v((4, 96, 128), F32), v((4, 96, 128), F32), v((96, 128), BF), v((NZ, 96, 128), BF), v((96, 128), F32),
            v((4, 96, 128), F32), v((2, 4, 4, 96, 128), F32),
            dma((9,)), dma((9,)), dma((2,)), dma((2,)), dma((6,)), dma((6,)), dma((4,)), dma((4,)),
            dma((4, 4)), dma((4, 3)), dma((4, 4)), dma((4, 3)), dma((7,)), dma((7,)),
        ],
        compiler_params=pltpu.CompilerParams(
            collective_id=0, has_side_effects=True, vmem_limit_bytes=67_000_000
        ),
    )(
        *rows,
        upstream_warm, upstream_cold, upstream_hot, saved_hot, saved_warm, saved_cold,
        weight_warm, weight_cold, weight_hot,
    )
    return pl.pallas_call(
        write_out,
        out_shape=results,
        in_specs=[anywhere] * 6,
        out_specs=(anywhere,) * 6,
        scratch_shapes=[v(a.shape, F32) for a in results] + [dma((36,))],
    )(*found)


def solution(mesh):
    both = ("wide", "narrow")
    placed = (
        P(both, None), P(both, None), P(both, None), P(both, None), P(both, None), P(None, both),
        P(), P(), P(),
        P(both, None), P(both, None), P(both, None), P(both), P(both), P(both),
    )
    return jax.shard_map(
        per_device,
        mesh=mesh,
        in_specs=placed,
        out_specs=(P(both, None), P(both, None), P(None, both), P(), P(), P()),
        check_vma=False,
    )
```

```python
import math

import jax
import jax.numpy as jnp
from jax import lax
from jax.experimental import pallas as pl
from jax.experimental.pallas import tpu as pltpu
from jax.sharding import PartitionSpec as P

MESH = pl.DeviceIdType.MESH
BF = jnp.bfloat16
F32 = jnp.float32
I32 = jnp.int32

NZ = 8
NP = 32
CAP = 16
LOOK = 2048
HOT = 1
COLD = 5
NT = (((1,), (1,)), ((), ()))
TN = (((0,), (0,)), ((), ()))
PIECE = 384


def dot(a, b, dims=(((1,), (0,)), ((), ()))):
    return lax.dot_general(a, b, dims, preferred_element_type=F32)


def iota(shape, dim):
    return lax.broadcasted_iota(I32, shape, dim)


def one(cond):
    return jnp.where(cond, 1.0, 0.0).astype(BF)


def kernel(
    factor,
    own_h, own_w, own_c, loc_h, loc_w, loc_c,
    a_up_w, a_up_c, a_up_h, a_sv_h, a_sv_w, a_sv_c, a_w_w, a_w_c, a_w_h,
    hbm_th, hbm_tw, hbm_tc, hbm_mh, hbm_mw, hbm_mc,
    out_th, out_tw, out_tc, out_mh, out_mw, out_mc,
    up_w, up_c, up_h, sv_h, sv_w, sv_c, w_w, w_c, w_h,
    term_w, term_c, term_h,
    tri, pick, slots, ls, lr, lz, zl,
    s, r, s_c, r_c, ohh, ring_l, ring_s, got_l, got_s,
    zw, zc, cs, xw, ohw, lows,
    mp, pair, part, zsum, apart, asum, bpart, bsum, total, zall, gall,
    in_sem, out_sem, lab_send, lab_recv, pl_send, pl_recv, z_send, z_recv,
    rl_send, rs_send, rl_recv, rs_recv, ar_send, ar_recv,
):
    wide, narrow = lax.axis_index("wide"), lax.axis_index("narrow")
    me_z, me_y = lax.div(wide, 4), lax.rem(wide, 4)
    me_x, me_c = lax.div(narrow, 2), lax.rem(narrow, 2)
    me_p = me_y * 8 + narrow
    other = (wide, me_x * 2 + 1 - me_c)

    def plane_dev(p):
        return (me_z * 4 + lax.div(p, 8), lax.rem(p, 8))

    def z_dev(z):
        return (z * 4 + me_y, narrow)

    def chip(i):
        x, y = me_x + lax.rem(i, 4), me_y + i + lax.div(i, 4)
        return lax.rem(y, 4) * 4 + lax.rem(x, 4)

    def at(z):
        return lax.rem(z + 2 * NZ - me_z - 3, NZ)

    def to_peers(send):
        send(me_p + 1 - 2 * me_c)

        @pl.loop(1, NP // 2)
        def _(i):
            send(chip(i) * 2)
            send(chip(i) * 2 + 1)

    def remote(src, dst, ssem, rsem, dev):
        return pltpu.make_async_remote_copy(
            src_ref=src, dst_ref=dst, send_sem=ssem, recv_sem=rsem, device_id=dev, device_id_type=MESH
        )

    def drain(ref, sem):
        pltpu.make_async_copy(ref, ref, sem).wait()

    loads = {}
    for n, (name, src, dst) in enumerate(
        (
            ("w_w", a_w_w, w_w), ("up_w", a_up_w, up_w), ("up_h", a_up_h, up_h), ("sv_h", a_sv_h, sv_h),
            ("sv_w", a_sv_w, sv_w), ("up_c", a_up_c, up_c), ("sv_c", a_sv_c, sv_c), ("w_h", a_w_h, w_h),
            ("w_c", a_w_c, w_c),
        )
    ):
        loads[name] = pltpu.make_async_copy(src, dst, in_sem.at[n])
        loads[name].start()

    barrier = pltpu.get_barrier_semaphore()

    @pl.loop(1, NP)
    def _(i):
        pl.semaphore_signal(barrier, inc=1, device_id=plane_dev(lax.rem(me_p + i, NP)), device_id_type=MESH)

    @pl.loop(1, NZ)
    def _(i):
        pl.semaphore_signal(barrier, inc=1, device_id=z_dev(lax.rem(me_z + i, NZ)), device_id_type=MESH)

    def exact(values):
        return values.astype(F32).astype(BF)

    def match(row, rows=256):
        return jnp.where(exact(iota((rows, row.shape[1]), 0)) == row, jnp.ones((), BF), jnp.zeros((), BF))

    def near(row, base):
        return exact(jnp.clip(row - base, -1, 256))

    def keys(b, own_ref, loc_ref):
        own, label = own_ref[...], loc_ref[...] + 1
        key = exact((own & 31) * 8 + (own >> 5))
        if b < 2:
            base = ((own & 31) * 8 + (((own >> 5) + (13 - me_z)) & 7)) * CAP
        else:
            base = (own & 31) * 128 + (((own >> 5) + me_p) & 7) * CAP
        high, low = exact(label >> 6), exact(label & 63)
        lane = exact(iota((128, 256), 0) & 15)
        none = jnp.zeros((), BF)
        run = jnp.zeros((256, 128), F32)
        both = jnp.zeros((256, 256), F32)
        for k in range(8):
            cols = slice(k * 256, (k + 1) * 256)
            hit = match(key[:, cols])
            count = dot(hit, tri[...])
            before = count[:, 0:256] + jnp.concatenate([run, run], axis=1)
            run = run + count[:, 256:384]
            place = jnp.sum(before * hit.astype(F32), axis=0, keepdims=True)
            slots[b, :, cols] = base[:, cols] + place.astype(I32)
            there = lane == place.astype(BF)
            parts = [jnp.where(there, high[:, cols], none), jnp.where(there, low[:, cols], none)]
            both += dot(hit, jnp.concatenate(parts, axis=0), NT)
        found = both[:, 0:128] * 64.0 + both[:, 128:]
        block = ((iota((256, 128), 0) & 7) + me_p) & 7
        found = jnp.where((iota((256, 128), 1) >> 4) == block, found, 0.0)
        ls[b] = jnp.sum(found.reshape(NP, NZ, 128), axis=1, keepdims=True).astype(I32)

    def project(up, w, term):
        @pl.loop(0, 2)
        def _(i):
            rows = pl.ds(pl.multiple_of(i * 1024, 1024), 1024)
            term[rows, :] = dot(up[rows, :], w[...], NT).astype(BF)

    def send_one(k, p):
        remote(s.at[k, p], r.at[k, me_p], pl_send.at[k], pl_recv.at[k], plane_dev(p)).start()

    def picks(b, q):
        for k in range(8):
            cols = slice(k * 256, (k + 1) * 256)
            pick[:, cols] = match(near(slots[b, :, cols], q * 256))

    def pack(b, term, first, chunks, extra, when):
        @pl.loop(0, NP // 2)
        def _(i):
            q = chip(i)
            picks(b, q)
            for n in range(0, chunks, 2):
                width = min(2, chunks - n)
                if width == 1:
                    res = dot(pick[:, :1024], term[:1024]) + dot(pick[:, 1024:], term[1024:])
                else:
                    res = dot(pick[...], term[:, n * 128:(n + width) * 128])
                res = res.astype(BF)
                for m in range(width):
                    s[first + n + m, pl.ds(q * 2, 2)] = res[:, m * 128:(m + 1) * 128].reshape(2, NZ, CAP, 128)

            @pl.when(i > 1)
            def _():
                last = chip(i - 1)
                send_one(first, last * 2)
                send_one(first, last * 2 + 1)

            pl.when(i == when)(extra)

        final = chip(NP // 2 - 1)
        pltpu.make_async_copy(s.at[first, me_p], r.at[first, me_p], pl_recv.at[first]).start()
        send_one(first, me_p + 1 - 2 * me_c)
        send_one(first, final * 2)
        send_one(first, final * 2 + 1)

    def pack_cold(part):
        if part == 0:
            loads["w_c"].wait()
            term_c[...] = dot(w_c[...], up_c[...], NT).astype(BF)

        @pl.loop(part * 4, part * 4 + 4)
        def _(i):
            q = chip(i)
            picks(2, q)
            res = dot(term_c[...], pick[...], NT).astype(BF)
            s_c[q * 2] = res[:, :128]
            s_c[q * 2 + 1] = res[:, 128:]

    def send_cold():
        pltpu.make_async_copy(s_c.at[me_p], r_c.at[me_p], pl_recv.at[COLD]).start()

        to_peers(
            lambda p: remote(
                s_c.at[p], r_c.at[me_p], pl_send.at[COLD], pl_recv.at[COLD], plane_dev(p)
            ).start()
        )

    def send_chunk(k):
        pltpu.make_async_copy(s.at[k, me_p], r.at[k, me_p], pl_recv.at[k]).start()

        to_peers(lambda p: send_one(k, p))

    def send_part(k, n, lo, hi):
        pltpu.make_async_copy(s.at[k, me_p, lo:hi], r.at[k, me_p, lo:hi], pl_recv.at[n]).start()
        to_peers(
            lambda p: remote(
                s.at[k, p, lo:hi], r.at[k, me_p, lo:hi], pl_send.at[n], pl_recv.at[n], plane_dev(p)
            ).start()
        )

    def send_labels(n, lo, hi):
        pltpu.make_async_copy(ls.at[lo:hi, me_p], lr.at[lo:hi, me_p], lab_recv.at[n]).start()

        to_peers(
            lambda p: remote(
                ls.at[lo:hi, p], lr.at[lo:hi, me_p], lab_send.at[n], lab_recv.at[n], plane_dev(p)
            ).start()
        )

    def keep(row, value):
        done = 0
        while done < value.shape[0]:
            half, inside = divmod(row + done, PIECE)
            upper, inside = divmod(inside, PIECE // 2)
            count = min(PIECE // 2 - inside, value.shape[0] - done)
            for lane in range(4):
                mp[half, upper * 4 + lane, inside:inside + count, :] = value[
                    done:done + count, lane * 128:(lane + 1) * 128
                ]
            done += count

    def mix_terms():
        for name in ("up_h", "sv_h", "sv_w", "up_c", "sv_c"):
            loads[name].wait()
        for m in range(4):
            keep(m * 128, dot(sv_h[:, m * 128:(m + 1) * 128], up_h[...], TN))
        keep(512, dot(sv_w[...], up_w[...], TN))
        keep(640, dot(sv_c[...], up_c[...]))
        keep(672, jnp.zeros((96, 512), F32))

    def mix_pair():
        remote(mp.at[1 - me_c], pair, ar_send.at[0], ar_recv.at[0], other).start()

    me_a = me_x + me_c * (me_y - me_x)
    me_b = me_y + me_c * (me_x - me_y)

    def a_dev(k):
        return (me_z * 4 + me_y + me_c * (k - me_y), (k + me_c * (me_x - k)) * 2 + me_c)

    def b_dev(k):
        return (me_z * 4 + k + me_c * (me_y - k), (me_x + me_c * (k - me_x)) * 2 + me_c)

    def spread(n, src_of, dst, dev, me, count):
        pltpu.make_async_copy(src_of(me), dst, ar_recv.at[n]).start()

        @pl.loop(1, count)
        def _(i):
            k = lax.rem(me + i, count)
            remote(src_of(k), dst, ar_send.at[n], ar_recv.at[n], dev(k)).start()

    def mix_z():
        drain(pair, ar_recv.at[0])
        for q in range(NZ):
            part[q] = (mp[me_c, q] + pair[q]).astype(BF)
        spread(1, lambda k: part.at[k], zsum.at[me_z], z_dev, me_z, NZ)

    def mix_a():
        drain(zsum, ar_recv.at[1])
        for k in range(4):
            rows = slice(k * 48, (k + 1) * 48)
            apart[k] = sum((zsum[z, rows].astype(F32) for z in range(1, NZ)), zsum[0, rows].astype(F32))
        spread(2, lambda k: apart.at[k], asum.at[me_a], a_dev, me_a, 4)

    def mix_b():
        drain(asum, ar_recv.at[2])
        bpart[...] = asum[0] + asum[1] + asum[2] + asum[3]
        spread(3, lambda k: bpart, bsum.at[me_b], b_dev, me_b, 4)

    def mix_z_back():
        drain(bsum, ar_recv.at[3])
        total[...] = (bsum[0] + bsum[1] + bsum[2] + bsum[3]) * factor
        spread(4, lambda k: total, zall.at[me_z], z_dev, me_z, NZ)

    def mix_a_back():
        drain(zall, ar_recv.at[4])
        spread(5, lambda k: zall, gall.at[me_c, me_a], a_dev, me_a, 4)

    def mix_pair_back():
        drain(gall.at[0], ar_recv.at[5])
        remote(gall.at[me_c], gall.at[me_c], ar_send.at[6], ar_recv.at[6], other).start()

    def mix_out():
        drain(gall.at[0], ar_recv.at[6])
        for half in range(2):
            for q in range(NZ):
                cols = slice((q % 4) * 128, (q % 4 + 1) * 128)
                for a in range(4):
                    value = gall[half, a, q]
                    row = half * PIECE + (q // 4) * (PIECE // 2) + a * 48
                    for lo, hi, out in ((0, 512, out_mh), (512, 640, out_mw), (640, 672, out_mc)):
                        begin, end = max(row, lo), min(row + 48, hi)
                        if begin < end:
                            out[begin - lo:end - lo, cols] = value[begin - row:end - row]

    def sort_labels(b):
        lz[b] = jnp.zeros((NZ, 8, 128), I32)
        block, z_at = iota((NZ, 128), 1) >> 4, iota((NZ, 128), 0)
        for j in range(4):
            row = jnp.zeros((NZ, 128), I32)
            for p in range(8):
                row = row + jnp.where(block == ((z_at + p) & 7), lr[b, 8 * j + p], 0)
            for z in range(NZ):
                lz[b, z, j:j + 1, :] = row[z:z + 1, :]

    def hot_rows():
        @pl.loop(0, NZ)
        def _(t):
            for j in range(4):
                row = lz[1, t, j:j + 1, :] - 1
                for half in range(2):
                    ohh[t, half * 256:(half + 1) * 256, j * 128:(j + 1) * 128] = match(near(row, half * 256))

    def labels_on(b, n):
        spread_z(lambda t: lz.at[b, t], zl.at[n, me_z], z_send.at[2 + n], z_recv.at[2 + n])

    def spread_z(src_of, dst, ssem, rsem):
        pltpu.make_async_copy(src_of(me_z), dst, rsem).start()

        @pl.loop(1, NZ)
        def _(i):
            t = lax.rem(me_z + i, NZ)
            remote(src_of(t), dst, ssem, rsem, z_dev(t)).start()

    def warm_on():
        drain(r.at[0], pl_recv.at[0])
        spread_z(lambda t: r.at[0, :, at(t)], zw.at[me_z], z_send.at[0], z_recv.at[0])

    def cold_on():
        drain(r_c, pl_recv.at[COLD])

        @pl.loop(0, NZ)
        def _(t):
            for j in range(4):
                parts = [
                    jnp.where((iota((32, 128), 1) >> 4) == ((t + p) & 7), r_c[8 * j + p].astype(F32), 0.0)
                    for p in range(8)
                ]
                cs[t, :, j * 128:(j + 1) * 128] = sum(parts).astype(BF)

        spread_z(lambda t: cs.at[t], zc.at[me_z], z_send.at[1], z_recv.at[1])

    def leave(n, src, dst):
        copy = pltpu.make_async_copy(src, dst, out_sem.at[n])
        copy.start()
        leaving.append(copy)

    leaving = []

    def partial(c, t):
        x = jnp.concatenate(
            [r[HOT + c, 8 * j + lax.rem(i + NZ - t, NZ), at(t)] for j in range(4) for i in range(8)], axis=0
        )
        return dot(ohh[t], x)

    def ring(c, step):
        way = 1 - 2 * lax.rem(me_c + c, 2)
        value = partial(c, lax.rem(me_z + NZ + way * (4 - step), NZ))
        if step:
            drain(got_l.at[c, step - 1], rl_recv.at[c, step - 1])
            value = value + got_l[c, step - 1].astype(F32)
        ring_l[c, step] = value.astype(BF)
        if step:
            value = partial(c, lax.rem(me_z + NZ - way * (4 - step), NZ))
            if step > 1:
                drain(got_s.at[c, step - 2], rs_recv.at[c, step - 2])
                value = value + got_s[c, step - 2].astype(F32)
            ring_s[c, step - 1] = value.astype(BF)
        remote(
            ring_l.at[c, step], got_l.at[c, step], rl_send.at[c, step], rl_recv.at[c, step],
            z_dev(lax.rem(me_z + NZ + way, NZ)),
        ).start()
        if step:
            remote(
                ring_s.at[c, step - 1], got_s.at[c, step - 1], rs_send.at[c, step - 1], rs_recv.at[c, step - 1],
                z_dev(lax.rem(me_z + NZ - way, NZ)),
            ).start()

    def ring_end(c):
        value = partial(c, me_z)
        drain(got_l.at[c, 3], rl_recv.at[c, 3])
        drain(got_s.at[c, 2], rs_recv.at[c, 2])
        cols = slice(c * 128, (c + 1) * 128)
        out_th[:, cols] = value + got_l[c, 3].astype(F32) + got_s[c, 2].astype(F32)
        leave(c, out_th.at[:, cols], hbm_th.at[:, cols])

    def arrive_part(n, lo, hi):
        drain(r.at[HOT + 3, :, lo:hi], pl_recv.at[n])

    def arrive(c):
        drain(r.at[HOT + c], pl_recv.at[HOT + c])

    def warm_table(half):
        if half == 0:
            drain(zw, z_recv.at[0])
            drain(zl.at[0], z_recv.at[2])

            @pl.loop(0, NZ)
            def _(z):
                for j in range(4):
                    rows = pl.ds(pl.multiple_of((z * 4 + j) * 128, 128), 128)
                    xw[rows, :] = jnp.concatenate(
                        [zw[z, 8 * j + lax.rem(i + NZ - me_z, NZ)] for i in range(8)], axis=0
                    )

        @pl.loop(half * 4, half * 4 + 4)
        def _(i):
            for z in range(NZ):
                for j in range(4):
                    k = (z * 4 + j) * 128
                    ohw[:, k:k + 128] = match(near(zl[0, z, j:j + 1, :] - 1, i * 256))
            res = dot(ohw[:, :2048], xw[:2048]) + dot(ohw[:, 2048:], xw[2048:])
            out_tw[pl.ds(pl.multiple_of(i * 256, 256), 256), :] = res

        if half:
            leave(4, out_tw, hbm_tw)

    def cold_table():
        drain(zc, z_recv.at[1])
        drain(zl.at[1], z_recv.at[3])
        for z in range(NZ):
            for j in range(4):
                k = (z * 4 + j) * 128
                lows[:, k:k + 128] = match(exact((zl[1, z, j:j + 1, :] - 1) & 127), 128)

        @pl.loop(0, 4)
        def _(h):
            for z in range(NZ):
                for j in range(4):
                    k = (z * 4 + j) * 128
                    high = near((zl[1, z, j:j + 1, :] - 1) >> 7, h * 8)
                    for i in range(8):
                        here = jnp.broadcast_to(high, (32, 128)) == jnp.full((), i, BF)
                        ohw[i * 32:(i + 1) * 32, k:k + 128] = jnp.where(
                            here, zc[z, :, j * 128:(j + 1) * 128], jnp.zeros((), BF)
                        )
            res = dot(ohw[:, :2048], lows[:, :2048], NT) + dot(ohw[:, 2048:], lows[:, 2048:], NT)
            for i in range(8):
                out_tc[:, pl.ds(pl.multiple_of(h * 1024 + i * 128, 128), 128)] = res[i * 32:(i + 1) * 32, :]

        leave(5, out_tc, hbm_tc)

    tri[:, 0:256] = one(iota((256, 256), 0) < iota((256, 256), 1))
    tri[:, 256:384] = jnp.ones((256, 128), BF)
    keys(0, own_w, loc_w)
    loads["w_w"].wait()
    loads["up_w"].wait()
    project(up_w, w_w, term_w)
    mix_terms()
    pl.semaphore_wait(barrier, NP - 1 + NZ - 1)
    mix_pair()
    pack(0, term_w, 0, 1, mix_z, 8)
    keys(1, own_h, loc_h)
    send_labels(0, 0, 2)
    loads["w_h"].wait()
    project(up_h, w_h, term_h)
    pack(1, term_h, HOT, 4, warm_on, 6)
    send_chunk(HOT + 1)
    drain(lr.at[0:2], lab_recv.at[0])
    sort_labels(0)
    labels_on(0, 0)
    sort_labels(1)
    hot_rows()
    keys(2, own_c, loc_c)
    pack_cold(0)
    arrive(0)
    ring(0, 0)
    send_chunk(HOT + 2)
    send_labels(1, 2, 3)
    mix_a()
    pack_cold(1)
    ring(0, 1)
    pack_cold(2)
    pack_cold(3)
    ring(0, 2)
    mix_b()
    arrive(1)
    ring(1, 0)
    send_cold()
    send_part(HOT + 3, HOT + 3, 0, 3)
    send_part(HOT + 3, 6, 3, 8)
    ring(0, 3)
    ring(1, 1)
    ring(1, 2)
    mix_z_back()
    arrive(2)
    ring(2, 0)
    ring(1, 3)
    warm_table(0)
    ring(2, 1)
    drain(lr.at[2], lab_recv.at[1])
    sort_labels(2)
    labels_on(2, 1)
    cold_on()
    arrive_part(HOT + 3, 0, 3)
    ring(3, 0)
    ring(2, 2)
    mix_a_back()
    ring(3, 1)
    ring(2, 3)
    ring_end(0)
    arrive_part(6, 3, 8)
    ring(3, 2)
    warm_table(1)
    mix_pair_back()
    ring_end(1)
    ring(3, 3)
    mix_out()
    leave(6, out_mh, hbm_mh)
    leave(7, out_mw, hbm_mw)
    leave(8, out_mc, hbm_mc)
    ring_end(2)
    cold_table()

    for k in range(4):
        drain(r.at[k, 0:NP - 1], pl_send.at[k])
    drain(r.at[HOT + 3, 0:NP - 1, 0:3], pl_send.at[HOT + 3])
    drain(r.at[HOT + 3, 0:NP - 1, 3:8], pl_send.at[6])
    drain(r_c.at[0:NP - 1], pl_send.at[COLD])
    drain(lr.at[0:2, 0:NP - 1], lab_send.at[0])
    drain(lr.at[2, 0:NP - 1], lab_send.at[1])
    drain(zw.at[0:NZ - 1], z_send.at[0])
    drain(zc.at[0:NZ - 1], z_send.at[1])
    drain(zl.at[0, 0:NZ - 1], z_send.at[2])
    drain(zl.at[1, 0:NZ - 1], z_send.at[3])
    drain(pair, ar_send.at[0])
    drain(zsum.at[0:NZ - 1], ar_send.at[1])
    drain(asum.at[0:3], ar_send.at[2])
    drain(bsum.at[0:3], ar_send.at[3])
    drain(zall.at[0:NZ - 1], ar_send.at[4])
    drain(gall.at[0, 0:3], ar_send.at[5])
    drain(gall.at[0], ar_send.at[6])
    for c in range(4):
        for step in range(4):
            drain(got_l.at[c, step], rl_send.at[c, step])
        for step in range(3):
            drain(got_s.at[c, step], rs_send.at[c, step])
    ring_end(3)
    for copy in leaving:
        copy.wait()


def write_out(*refs):
    ins, outs, rooms, (sem,) = refs[:6], refs[6:12], refs[12:18], refs[18:]
    copies = []
    n = 0
    for src, room, dst in zip(ins, rooms, outs):
        cuts = 4 if src.shape[0] >= 256 else 1
        rows = src.shape[0] // cuts
        for k in range(cuts):
            here = pl.ds(k * rows, rows)
            first = pltpu.make_async_copy(src.at[here], room.at[here], sem.at[n])
            second = pltpu.make_async_copy(room.at[here], dst.at[here], sem.at[n + 1])
            first.start()
            copies.append((first, second))
            n += 2
    for first, second in copies:
        first.wait()
        second.start()
    for _, second in copies:
        second.wait()


def per_device(
    upstream_hot, upstream_warm, upstream_cold, saved_hot, saved_warm, saved_cold,
    weight_hot, weight_warm, weight_cold, owner_hot, owner_warm, owner_cold,
    local_hot, local_warm, local_cold,
):
    devices = lax.axis_size("wide") * lax.axis_size("narrow")
    factor = 1.0 / math.sqrt(LOOK * devices)
    rows = [a.reshape(1, LOOK) for a in (owner_hot, owner_warm, owner_cold, local_hot, local_warm, local_cold)]
    anywhere = pl.BlockSpec(memory_space=pl.ANY)
    near = pl.BlockSpec(memory_space=pltpu.VMEM)
    dma = pltpu.SemaphoreType.DMA
    v = pltpu.VMEM
    results = tuple(
        jax.ShapeDtypeStruct(shape, F32)
        for shape in ((512, 512), (2048, 128), (32, 4096), (512, 512), (128, 512), (32, 512))
    )

    def body(*refs):
        kernel(factor, *refs)

    found = pl.pallas_call(
        body,
        out_shape=results,
        in_specs=[near] * 6 + [anywhere] * 9,
        out_specs=(anywhere,) * 6,
        scratch_shapes=[
            *(v(a.shape, F32) for a in results),
            v((2048, 512), BF), v((2048, 512), BF), v((2048, 512), BF),
            v((2048, 512), BF), v((2048, 128), BF), v((32, 2048), BF),
            v((128, 512), BF), v((32, 512), BF), v((512, 512), BF),
            v((2048, 128), BF), v((32, 2048), BF), v((2048, 512), BF),
            v((256, 384), BF), v((256, 2048), BF), v((3, 1, 2048), I32),
            v((3, NP, 1, 128), I32), v((3, NP, 1, 128), I32), v((3, NZ, 8, 128), I32), v((2, NZ, 8, 128), I32),
            v((5, NP, NZ, CAP, 128), BF), v((5, NP, NZ, CAP, 128), BF), v((NP, 32, 128), BF), v((NP, 32, 128), BF),
            v((NZ, 512, 512), BF),
            v((4, 4, 512, 128), BF), v((4, 3, 512, 128), BF), v((4, 4, 512, 128), BF), v((4, 3, 512, 128), BF),
            v((NZ, NP, CAP, 128), BF), v((NZ, 32, 512), BF), v((NZ, 32, 512), BF),
            v((4096, 128), BF), v((256, 4096), BF), v((128, 4096), BF),
            v((2, NZ, PIECE // 2, 128), F32), v((NZ, PIECE // 2, 128), F32), v((NZ, PIECE // 2, 128), BF),
            v((NZ, PIECE // 2, 128), BF), v((4, 48, 128), F32), v((4, 48, 128), F32), v((48, 128), F32),
            v((4, 48, 128), F32), v((48, 128), F32), v((NZ, 48, 128), F32), v((2, 4, NZ, 48, 128), F32),
            dma((9,)), dma((9,)), dma((2,)), dma((2,)), dma((7,)), dma((7,)), dma((4,)), dma((4,)),
            dma((4, 4)), dma((4, 3)), dma((4, 4)), dma((4, 3)), dma((7,)), dma((7,)),
        ],
        compiler_params=pltpu.CompilerParams(
            collective_id=0, has_side_effects=True, vmem_limit_bytes=67_000_000
        ),
    )(
        *rows,
        upstream_warm, upstream_cold, upstream_hot, saved_hot, saved_warm, saved_cold,
        weight_warm, weight_cold, weight_hot,
    )
    return pl.pallas_call(
        write_out,
        out_shape=results,
        in_specs=[anywhere] * 6,
        out_specs=(anywhere,) * 6,
        scratch_shapes=[v(a.shape, F32) for a in results] + [dma((36,))],
    )(*found)


def solution(mesh):
    both = ("wide", "narrow")
    placed = (
        P(both, None), P(both, None), P(both, None), P(both, None), P(both, None), P(None, both),
        P(), P(), P(),
        P(both, None), P(both, None), P(both, None), P(both), P(both), P(both),
    )
    return jax.shard_map(
        per_device,
        mesh=mesh,
        in_specs=placed,
        out_specs=(P(both, None), P(both, None), P(None, both), P(), P(), P()),
        check_vma=False,
    )
```

```python
import math

import jax
import jax.numpy as jnp
from jax import lax
from jax.experimental import pallas as pl
from jax.experimental.pallas import tpu as pltpu
from jax.sharding import PartitionSpec as P

MESH = pl.DeviceIdType.MESH
BF = jnp.bfloat16
F32 = jnp.float32
I32 = jnp.int32

NZ = 8
NP = 32
CAP = 16
LOOK = 2048
HOT = 1
COLD = 5
NT = (((1,), (1,)), ((), ()))
TN = (((0,), (0,)), ((), ()))
PIECE = 384


def dot(a, b, dims=(((1,), (0,)), ((), ()))):
    return lax.dot_general(a, b, dims, preferred_element_type=F32)


def iota(shape, dim):
    return lax.broadcasted_iota(I32, shape, dim)


def one(cond):
    return jnp.where(cond, 1.0, 0.0).astype(BF)


def kernel(
    factor,
    own_h, own_w, own_c, loc_h, loc_w, loc_c,
    a_up_w, a_up_c, a_up_h, a_sv_h, a_sv_w, a_sv_c, a_w_w, a_w_c, a_w_h,
    hbm_th, hbm_tw, hbm_tc, hbm_mh, hbm_mw, hbm_mc,
    out_th, out_tw, out_tc, out_mh, out_mw, out_mc,
    up_w, up_c, up_h, sv_h, sv_w, sv_c, w_w, w_c, w_h,
    term_w, term_c, term_h,
    tri, pick, slots, ls, lr, lz, zl,
    s, r, s_c, r_c, ohh, ring_l, ring_s, got_l, got_s,
    zw, ws, zc, cs, xw, ohw, lows,
    mp, pair, part, zsum, apart, asum, bpart, bsum, total, zall, gall,
    in_sem, out_sem, lab_send, lab_recv, pl_send, pl_recv, z_send, z_recv,
    rl_send, rs_send, rl_recv, rs_recv, ar_send, ar_recv,
):
    wide, narrow = lax.axis_index("wide"), lax.axis_index("narrow")
    me_z, me_y = lax.div(wide, 4), lax.rem(wide, 4)
    me_x, me_c = lax.div(narrow, 2), lax.rem(narrow, 2)
    me_p = me_y * 8 + narrow
    other = (wide, me_x * 2 + 1 - me_c)

    def plane_dev(p):
        return (me_z * 4 + lax.div(p, 8), lax.rem(p, 8))

    def z_dev(z):
        return (z * 4 + me_y, narrow)

    def chip(i):
        x, y = me_x + lax.rem(i, 4), me_y + i + lax.div(i, 4)
        return lax.rem(y, 4) * 4 + lax.rem(x, 4)

    def at(z):
        return lax.rem(z + 2 * NZ - me_z - 3, NZ)

    def to_peers(send):
        send(me_p + 1 - 2 * me_c)

        @pl.loop(1, NP // 2)
        def _(i):
            send(chip(i) * 2)
            send(chip(i) * 2 + 1)

    def remote(src, dst, ssem, rsem, dev):
        return pltpu.make_async_remote_copy(
            src_ref=src, dst_ref=dst, send_sem=ssem, recv_sem=rsem, device_id=dev, device_id_type=MESH
        )

    def drain(ref, sem):
        pltpu.make_async_copy(ref, ref, sem).wait()

    loads = {}
    for n, (name, src, dst) in enumerate(
        (
            ("w_w", a_w_w, w_w), ("up_w", a_up_w, up_w), ("up_h", a_up_h, up_h), ("sv_h", a_sv_h, sv_h),
            ("sv_w", a_sv_w, sv_w), ("up_c", a_up_c, up_c), ("sv_c", a_sv_c, sv_c), ("w_h", a_w_h, w_h),
            ("w_c", a_w_c, w_c),
        )
    ):
        loads[name] = pltpu.make_async_copy(src, dst, in_sem.at[n])
        loads[name].start()

    barrier = pltpu.get_barrier_semaphore()

    @pl.loop(1, NP)
    def _(i):
        pl.semaphore_signal(barrier, inc=1, device_id=plane_dev(lax.rem(me_p + i, NP)), device_id_type=MESH)

    @pl.loop(1, NZ)
    def _(i):
        pl.semaphore_signal(barrier, inc=1, device_id=z_dev(lax.rem(me_z + i, NZ)), device_id_type=MESH)

    def exact(values):
        return values.astype(F32).astype(BF)

    def match(row, rows=256):
        return jnp.where(exact(iota((rows, row.shape[1]), 0)) == row, jnp.ones((), BF), jnp.zeros((), BF))

    def near(row, base):
        return exact(jnp.clip(row - base, -1, 256))

    def keys(b, own_ref, loc_ref):
        own, label = own_ref[...], loc_ref[...] + 1
        key = exact((own & 31) * 8 + (own >> 5))
        if b < 2:
            base = ((own & 31) * 8 + (((own >> 5) + (13 - me_z)) & 7)) * CAP
        else:
            base = (own & 31) * 128 + (((own >> 5) + me_p) & 7) * CAP
        high, low = exact(label >> 6), exact(label & 63)
        lane = exact(iota((128, 256), 0) & 15)
        none = jnp.zeros((), BF)
        run = jnp.zeros((256, 128), F32)
        both = jnp.zeros((256, 256), F32)
        for k in range(8):
            cols = slice(k * 256, (k + 1) * 256)
            hit = match(key[:, cols])
            count = dot(hit, tri[...])
            before = count[:, 0:256] + jnp.concatenate([run, run], axis=1)
            run = run + count[:, 256:384]
            place = jnp.sum(before * hit.astype(F32), axis=0, keepdims=True)
            slots[b, :, cols] = base[:, cols] + place.astype(I32)
            there = lane == place.astype(BF)
            parts = [jnp.where(there, high[:, cols], none), jnp.where(there, low[:, cols], none)]
            both += dot(hit, jnp.concatenate(parts, axis=0), NT)
        found = both[:, 0:128] * 64.0 + both[:, 128:]
        block = ((iota((256, 128), 0) & 7) + me_p) & 7
        found = jnp.where((iota((256, 128), 1) >> 4) == block, found, 0.0)
        ls[b] = jnp.sum(found.reshape(NP, NZ, 128), axis=1, keepdims=True).astype(I32)

    def project(up, w, term):
        @pl.loop(0, 2)
        def _(i):
            rows = pl.ds(pl.multiple_of(i * 1024, 1024), 1024)
            term[rows, :] = dot(up[rows, :], w[...], NT).astype(BF)

    def send_one(k, p):
        remote(s.at[k, p], r.at[k, me_p], pl_send.at[k], pl_recv.at[k], plane_dev(p)).start()

    def picks(b, q):
        for k in range(8):
            cols = slice(k * 256, (k + 1) * 256)
            pick[:, cols] = match(near(slots[b, :, cols], q * 256))

    def pack(b, term, first, chunks, extra, when):
        @pl.loop(0, NP // 2)
        def _(i):
            q = chip(i)
            picks(b, q)
            for n in range(0, chunks, 2):
                width = min(2, chunks - n)
                if width == 1:
                    res = dot(pick[:, :1024], term[:1024]) + dot(pick[:, 1024:], term[1024:])
                else:
                    res = dot(pick[...], term[:, n * 128:(n + width) * 128])
                res = res.astype(BF)
                for m in range(width):
                    s[first + n + m, pl.ds(q * 2, 2)] = res[:, m * 128:(m + 1) * 128].reshape(2, NZ, CAP, 128)

            @pl.when(i > 1)
            def _():
                last = chip(i - 1)
                send_one(first, last * 2)
                send_one(first, last * 2 + 1)

            pl.when(i == when)(extra)

        final = chip(NP // 2 - 1)
        pltpu.make_async_copy(s.at[first, me_p], r.at[first, me_p], pl_recv.at[first]).start()
        send_one(first, me_p + 1 - 2 * me_c)
        send_one(first, final * 2)
        send_one(first, final * 2 + 1)

    def pack_cold(part):
        if part == 0:
            loads["w_c"].wait()
            term_c[...] = dot(w_c[...], up_c[...], NT).astype(BF)

        @pl.loop(part * 4, part * 4 + 4)
        def _(i):
            q = chip(i)
            picks(2, q)
            res = dot(term_c[...], pick[...], NT).astype(BF)
            s_c[q * 2] = res[:, :128]
            s_c[q * 2 + 1] = res[:, 128:]

    def send_cold():
        pltpu.make_async_copy(s_c.at[me_p], r_c.at[me_p], pl_recv.at[COLD]).start()

        to_peers(
            lambda p: remote(
                s_c.at[p], r_c.at[me_p], pl_send.at[COLD], pl_recv.at[COLD], plane_dev(p)
            ).start()
        )

    def send_chunk(k):
        pltpu.make_async_copy(s.at[k, me_p], r.at[k, me_p], pl_recv.at[k]).start()

        to_peers(lambda p: send_one(k, p))

    def send_part(k, n, lo, hi):
        pltpu.make_async_copy(s.at[k, me_p, lo:hi], r.at[k, me_p, lo:hi], pl_recv.at[n]).start()
        to_peers(
            lambda p: remote(
                s.at[k, p, lo:hi], r.at[k, me_p, lo:hi], pl_send.at[n], pl_recv.at[n], plane_dev(p)
            ).start()
        )

    def send_labels(n, lo, hi):
        pltpu.make_async_copy(ls.at[lo:hi, me_p], lr.at[lo:hi, me_p], lab_recv.at[n]).start()

        to_peers(
            lambda p: remote(
                ls.at[lo:hi, p], lr.at[lo:hi, me_p], lab_send.at[n], lab_recv.at[n], plane_dev(p)
            ).start()
        )

    def keep(row, value):
        done = 0
        while done < value.shape[0]:
            half, inside = divmod(row + done, PIECE)
            upper, inside = divmod(inside, PIECE // 2)
            count = min(PIECE // 2 - inside, value.shape[0] - done)
            for lane in range(4):
                mp[half, upper * 4 + lane, inside:inside + count, :] = value[
                    done:done + count, lane * 128:(lane + 1) * 128
                ]
            done += count

    def mix_terms():
        for name in ("up_h", "sv_h", "sv_w", "up_c", "sv_c"):
            loads[name].wait()
        for m in range(4):
            keep(m * 128, dot(sv_h[:, m * 128:(m + 1) * 128], up_h[...], TN))
        keep(512, dot(sv_w[...], up_w[...], TN))
        keep(640, dot(sv_c[...], up_c[...]))
        keep(672, jnp.zeros((96, 512), F32))

    def mix_pair():
        remote(mp.at[1 - me_c], pair, ar_send.at[0], ar_recv.at[0], other).start()

    me_a = me_x + me_c * (me_y - me_x)
    me_b = me_y + me_c * (me_x - me_y)

    def a_dev(k):
        return (me_z * 4 + me_y + me_c * (k - me_y), (k + me_c * (me_x - k)) * 2 + me_c)

    def b_dev(k):
        return (me_z * 4 + k + me_c * (me_y - k), (me_x + me_c * (k - me_x)) * 2 + me_c)

    def spread(n, src_of, dst, dev, me, count):
        pltpu.make_async_copy(src_of(me), dst, ar_recv.at[n]).start()

        @pl.loop(1, count)
        def _(i):
            k = lax.rem(me + i, count)
            remote(src_of(k), dst, ar_send.at[n], ar_recv.at[n], dev(k)).start()

    def mix_z():
        drain(pair, ar_recv.at[0])
        for q in range(NZ):
            part[q] = (mp[me_c, q] + pair[q]).astype(BF)
        spread(1, lambda k: part.at[k], zsum.at[me_z], z_dev, me_z, NZ)

    def mix_a():
        drain(zsum, ar_recv.at[1])
        for k in range(4):
            rows = slice(k * 48, (k + 1) * 48)
            apart[k] = sum((zsum[z, rows].astype(F32) for z in range(1, NZ)), zsum[0, rows].astype(F32))
        spread(2, lambda k: apart.at[k], asum.at[me_a], a_dev, me_a, 4)

    def mix_b():
        drain(asum, ar_recv.at[2])
        bpart[...] = asum[0] + asum[1] + asum[2] + asum[3]
        spread(3, lambda k: bpart, bsum.at[me_b], b_dev, me_b, 4)

    def mix_z_back():
        drain(bsum, ar_recv.at[3])
        total[...] = (bsum[0] + bsum[1] + bsum[2] + bsum[3]) * factor
        spread(4, lambda k: total, zall.at[me_z], z_dev, me_z, NZ)

    def mix_a_back():
        drain(zall, ar_recv.at[4])
        spread(5, lambda k: zall, gall.at[me_c, me_a], a_dev, me_a, 4)

    def mix_pair_back():
        drain(gall.at[0], ar_recv.at[5])
        remote(gall.at[me_c], gall.at[me_c], ar_send.at[6], ar_recv.at[6], other).start()

    def mix_out():
        drain(gall.at[0], ar_recv.at[6])
        for half in range(2):
            for q in range(NZ):
                cols = slice((q % 4) * 128, (q % 4 + 1) * 128)
                for a in range(4):
                    value = gall[half, a, q]
                    row = half * PIECE + (q // 4) * (PIECE // 2) + a * 48
                    for lo, hi, out in ((0, 512, out_mh), (512, 640, out_mw), (640, 672, out_mc)):
                        begin, end = max(row, lo), min(row + 48, hi)
                        if begin < end:
                            out[begin - lo:end - lo, cols] = value[begin - row:end - row]

    def sort_labels(b):
        lz[b] = jnp.zeros((NZ, 8, 128), I32)
        block, z_at = iota((NZ, 128), 1) >> 4, iota((NZ, 128), 0)
        for j in range(4):
            row = jnp.zeros((NZ, 128), I32)
            for p in range(8):
                row = row + jnp.where(block == ((z_at + p) & 7), lr[b, 8 * j + p], 0)
            for z in range(NZ):
                lz[b, z, j:j + 1, :] = row[z:z + 1, :]

    def hot_rows():
        @pl.loop(0, NZ)
        def _(t):
            for j in range(4):
                row = lz[1, t, j:j + 1, :] - 1
                for half in range(2):
                    ohh[t, half * 256:(half + 1) * 256, j * 128:(j + 1) * 128] = match(near(row, half * 256))

    def labels_on(b, n):
        spread_z(lambda t: lz.at[b, t], zl.at[n, me_z], z_send.at[2 + n], z_recv.at[2 + n])

    def spread_z(src_of, dst, ssem, rsem):
        pltpu.make_async_copy(src_of(me_z), dst, rsem).start()

        @pl.loop(1, NZ)
        def _(i):
            t = lax.rem(me_z + i, NZ)
            remote(src_of(t), dst, ssem, rsem, z_dev(t)).start()

    def warm_on():
        drain(r.at[0], pl_recv.at[0])

        @pl.loop(0, NZ)
        def _(i):
            t = lax.rem(me_z + i, NZ)
            for p in range(NP):
                ws[t, p] = r[0, p, at(t)]

        spread_z(lambda t: ws.at[t], zw.at[me_z], z_send.at[0], z_recv.at[0])

    def cold_on():
        drain(r_c, pl_recv.at[COLD])

        @pl.loop(0, NZ)
        def _(t):
            for j in range(4):
                parts = [
                    jnp.where((iota((32, 128), 1) >> 4) == ((t + p) & 7), r_c[8 * j + p].astype(F32), 0.0)
                    for p in range(8)
                ]
                cs[t, :, j * 128:(j + 1) * 128] = sum(parts).astype(BF)

        spread_z(lambda t: cs.at[t], zc.at[me_z], z_send.at[1], z_recv.at[1])

    def leave(n, src, dst):
        copy = pltpu.make_async_copy(src, dst, out_sem.at[n])
        copy.start()
        leaving.append(copy)

    leaving = []

    def partial(c, t):
        x = jnp.concatenate(
            [r[HOT + c, 8 * j + lax.rem(i + NZ - t, NZ), at(t)] for j in range(4) for i in range(8)], axis=0
        )
        return dot(ohh[t], x)

    def ring(c, step):
        way = 1 - 2 * lax.rem(me_c + c, 2)
        value = partial(c, lax.rem(me_z + NZ + way * (4 - step), NZ))
        if step:
            drain(got_l.at[c, step - 1], rl_recv.at[c, step - 1])
            value = value + got_l[c, step - 1].astype(F32)
        ring_l[c, step] = value.astype(BF)
        if step:
            value = partial(c, lax.rem(me_z + NZ - way * (4 - step), NZ))
            if step > 1:
                drain(got_s.at[c, step - 2], rs_recv.at[c, step - 2])
                value = value + got_s[c, step - 2].astype(F32)
            ring_s[c, step - 1] = value.astype(BF)
        remote(
            ring_l.at[c, step], got_l.at[c, step], rl_send.at[c, step], rl_recv.at[c, step],
            z_dev(lax.rem(me_z + NZ + way, NZ)),
        ).start()
        if step:
            remote(
                ring_s.at[c, step - 1], got_s.at[c, step - 1], rs_send.at[c, step - 1], rs_recv.at[c, step - 1],
                z_dev(lax.rem(me_z + NZ - way, NZ)),
            ).start()

    def ring_end(c):
        value = partial(c, me_z)
        drain(got_l.at[c, 3], rl_recv.at[c, 3])
        drain(got_s.at[c, 2], rs_recv.at[c, 2])
        cols = slice(c * 128, (c + 1) * 128)
        out_th[:, cols] = value + got_l[c, 3].astype(F32) + got_s[c, 2].astype(F32)
        leave(c, out_th.at[:, cols], hbm_th.at[:, cols])

    def arrive_part(n, lo, hi):
        drain(r.at[HOT + 3, :, lo:hi], pl_recv.at[n])

    def arrive(c):
        drain(r.at[HOT + c], pl_recv.at[HOT + c])

    def warm_table(half):
        if half == 0:
            drain(zw, z_recv.at[0])
            drain(zl.at[0], z_recv.at[2])

            @pl.loop(0, NZ)
            def _(z):
                for j in range(4):
                    rows = pl.ds(pl.multiple_of((z * 4 + j) * 128, 128), 128)
                    xw[rows, :] = jnp.concatenate(
                        [zw[z, 8 * j + lax.rem(i + NZ - me_z, NZ)] for i in range(8)], axis=0
                    )

        @pl.loop(half * 4, half * 4 + 4)
        def _(i):
            for z in range(NZ):
                for j in range(4):
                    k = (z * 4 + j) * 128
                    ohw[:, k:k + 128] = match(near(zl[0, z, j:j + 1, :] - 1, i * 256))
            res = dot(ohw[:, :2048], xw[:2048]) + dot(ohw[:, 2048:], xw[2048:])
            out_tw[pl.ds(pl.multiple_of(i * 256, 256), 256), :] = res

        if half:
            leave(4, out_tw, hbm_tw)

    def cold_table():
        drain(zc, z_recv.at[1])
        drain(zl.at[1], z_recv.at[3])
        for z in range(NZ):
            for j in range(4):
                k = (z * 4 + j) * 128
                lows[:, k:k + 128] = match(exact((zl[1, z, j:j + 1, :] - 1) & 127), 128)

        @pl.loop(0, 4)
        def _(h):
            for z in range(NZ):
                for j in range(4):
                    k = (z * 4 + j) * 128
                    high = near((zl[1, z, j:j + 1, :] - 1) >> 7, h * 8)
                    for i in range(8):
                        here = jnp.broadcast_to(high, (32, 128)) == jnp.full((), i, BF)
                        ohw[i * 32:(i + 1) * 32, k:k + 128] = jnp.where(
                            here, zc[z, :, j * 128:(j + 1) * 128], jnp.zeros((), BF)
                        )
            res = dot(ohw[:, :2048], lows[:, :2048], NT) + dot(ohw[:, 2048:], lows[:, 2048:], NT)
            for i in range(8):
                out_tc[:, pl.ds(pl.multiple_of(h * 1024 + i * 128, 128), 128)] = res[i * 32:(i + 1) * 32, :]

        leave(5, out_tc, hbm_tc)

    tri[:, 0:256] = one(iota((256, 256), 0) < iota((256, 256), 1))
    tri[:, 256:384] = jnp.ones((256, 128), BF)
    keys(0, own_w, loc_w)
    loads["w_w"].wait()
    loads["up_w"].wait()
    project(up_w, w_w, term_w)
    mix_terms()
    pl.semaphore_wait(barrier, NP - 1 + NZ - 1)
    mix_pair()
    pack(0, term_w, 0, 1, mix_z, 8)
    keys(1, own_h, loc_h)
    send_labels(0, 0, 2)
    loads["w_h"].wait()
    project(up_h, w_h, term_h)
    pack(1, term_h, HOT, 4, warm_on, 6)
    send_chunk(HOT + 1)
    drain(lr.at[0:2], lab_recv.at[0])
    sort_labels(0)
    labels_on(0, 0)
    sort_labels(1)
    hot_rows()
    keys(2, own_c, loc_c)
    pack_cold(0)
    arrive(0)
    ring(0, 0)
    send_chunk(HOT + 2)
    send_labels(1, 2, 3)
    mix_a()
    pack_cold(1)
    ring(0, 1)
    pack_cold(2)
    pack_cold(3)
    ring(0, 2)
    arrive(1)
    ring(1, 0)
    send_cold()
    send_part(HOT + 3, HOT + 3, 0, 3)
    send_part(HOT + 3, 6, 3, 8)
    mix_b()
    ring(0, 3)
    ring(1, 1)
    ring(1, 2)
    mix_z_back()
    arrive(2)
    ring(2, 0)
    ring(1, 3)
    warm_table(0)
    ring(2, 1)
    drain(lr.at[2], lab_recv.at[1])
    sort_labels(2)
    labels_on(2, 1)
    cold_on()
    arrive_part(HOT + 3, 0, 3)
    ring(3, 0)
    ring(2, 2)
    mix_a_back()
    ring(3, 1)
    ring(2, 3)
    ring_end(0)
    arrive_part(6, 3, 8)
    ring(3, 2)
    warm_table(1)
    mix_pair_back()
    ring_end(1)
    ring(3, 3)
    mix_out()
    leave(6, out_mh, hbm_mh)
    leave(7, out_mw, hbm_mw)
    leave(8, out_mc, hbm_mc)
    ring_end(2)
    cold_table()

    for k in range(4):
        drain(r.at[k, 0:NP - 1], pl_send.at[k])
    drain(r.at[HOT + 3, 0:NP - 1, 0:3], pl_send.at[HOT + 3])
    drain(r.at[HOT + 3, 0:NP - 1, 3:8], pl_send.at[6])
    drain(r_c.at[0:NP - 1], pl_send.at[COLD])
    drain(lr.at[0:2, 0:NP - 1], lab_send.at[0])
    drain(lr.at[2, 0:NP - 1], lab_send.at[1])
    drain(zw.at[0:NZ - 1], z_send.at[0])
    drain(zc.at[0:NZ - 1], z_send.at[1])
    drain(zl.at[0, 0:NZ - 1], z_send.at[2])
    drain(zl.at[1, 0:NZ - 1], z_send.at[3])
    drain(pair, ar_send.at[0])
    drain(zsum.at[0:NZ - 1], ar_send.at[1])
    drain(asum.at[0:3], ar_send.at[2])
    drain(bsum.at[0:3], ar_send.at[3])
    drain(zall.at[0:NZ - 1], ar_send.at[4])
    drain(gall.at[0, 0:3], ar_send.at[5])
    drain(gall.at[0], ar_send.at[6])
    for c in range(4):
        for step in range(4):
            drain(got_l.at[c, step], rl_send.at[c, step])
        for step in range(3):
            drain(got_s.at[c, step], rs_send.at[c, step])
    ring_end(3)
    for copy in leaving:
        copy.wait()


def write_out(*refs):
    ins, outs, rooms, (sem,) = refs[:6], refs[6:12], refs[12:18], refs[18:]
    copies = []
    n = 0
    for src, room, dst in zip(ins, rooms, outs):
        cuts = 4 if src.shape[0] >= 256 else 1
        rows = src.shape[0] // cuts
        for k in range(cuts):
            here = pl.ds(k * rows, rows)
            first = pltpu.make_async_copy(src.at[here], room.at[here], sem.at[n])
            second = pltpu.make_async_copy(room.at[here], dst.at[here], sem.at[n + 1])
            first.start()
            copies.append((first, second))
            n += 2
    for first, second in copies:
        first.wait()
        second.start()
    for _, second in copies:
        second.wait()


def per_device(
    upstream_hot, upstream_warm, upstream_cold, saved_hot, saved_warm, saved_cold,
    weight_hot, weight_warm, weight_cold, owner_hot, owner_warm, owner_cold,
    local_hot, local_warm, local_cold,
):
    devices = lax.axis_size("wide") * lax.axis_size("narrow")
    factor = 1.0 / math.sqrt(LOOK * devices)
    rows = [a.reshape(1, LOOK) for a in (owner_hot, owner_warm, owner_cold, local_hot, local_warm, local_cold)]
    anywhere = pl.BlockSpec(memory_space=pl.ANY)
    near = pl.BlockSpec(memory_space=pltpu.VMEM)
    dma = pltpu.SemaphoreType.DMA
    v = pltpu.VMEM
    results = tuple(
        jax.ShapeDtypeStruct(shape, F32)
        for shape in ((512, 512), (2048, 128), (32, 4096), (512, 512), (128, 512), (32, 512))
    )

    def body(*refs):
        kernel(factor, *refs)

    found = pl.pallas_call(
        body,
        out_shape=results,
        in_specs=[near] * 6 + [anywhere] * 9,
        out_specs=(anywhere,) * 6,
        scratch_shapes=[
            *(v(a.shape, F32) for a in results),
            v((2048, 512), BF), v((2048, 512), BF), v((2048, 512), BF),
            v((2048, 512), BF), v((2048, 128), BF), v((32, 2048), BF),
            v((128, 512), BF), v((32, 512), BF), v((512, 512), BF),
            v((2048, 128), BF), v((32, 2048), BF), v((2048, 512), BF),
            v((256, 384), BF), v((256, 2048), BF), v((3, 1, 2048), I32),
            v((3, NP, 1, 128), I32), v((3, NP, 1, 128), I32), v((3, NZ, 8, 128), I32), v((2, NZ, 8, 128), I32),
            v((5, NP, NZ, CAP, 128), BF), v((5, NP, NZ, CAP, 128), BF), v((NP, 32, 128), BF), v((NP, 32, 128), BF),
            v((NZ, 512, 512), BF),
            v((4, 4, 512, 128), BF), v((4, 3, 512, 128), BF), v((4, 4, 512, 128), BF), v((4, 3, 512, 128), BF),
            v((NZ, NP, CAP, 128), BF), v((NZ, NP, CAP, 128), BF), v((NZ, 32, 512), BF), v((NZ, 32, 512), BF),
            v((4096, 128), BF), v((256, 4096), BF), v((128, 4096), BF),
            v((2, NZ, PIECE // 2, 128), F32), v((NZ, PIECE // 2, 128), F32), v((NZ, PIECE // 2, 128), BF),
            v((NZ, PIECE // 2, 128), BF), v((4, 48, 128), F32), v((4, 48, 128), F32), v((48, 128), F32),
            v((4, 48, 128), F32), v((48, 128), F32), v((NZ, 48, 128), F32), v((2, 4, NZ, 48, 128), F32),
            dma((9,)), dma((9,)), dma((2,)), dma((2,)), dma((7,)), dma((7,)), dma((4,)), dma((4,)),
            dma((4, 4)), dma((4, 3)), dma((4, 4)), dma((4, 3)), dma((7,)), dma((7,)),
        ],
        compiler_params=pltpu.CompilerParams(
            collective_id=0, has_side_effects=True, vmem_limit_bytes=67_000_000
        ),
    )(
        *rows,
        upstream_warm, upstream_cold, upstream_hot, saved_hot, saved_warm, saved_cold,
        weight_warm, weight_cold, weight_hot,
    )
    return pl.pallas_call(
        write_out,
        out_shape=results,
        in_specs=[anywhere] * 6,
        out_specs=(anywhere,) * 6,
        scratch_shapes=[v(a.shape, F32) for a in results] + [dma((36,))],
    )(*found)


def solution(mesh):
    both = ("wide", "narrow")
    placed = (
        P(both, None), P(both, None), P(both, None), P(both, None), P(both, None), P(None, both),
        P(), P(), P(),
        P(both, None), P(both, None), P(both, None), P(both), P(both), P(both),
    )
    return jax.shard_map(
        per_device,
        mesh=mesh,
        in_specs=placed,
        out_specs=(P(both, None), P(both, None), P(None, both), P(), P(), P()),
        check_vma=False,
    )
```
